32 devices in a mesh: grp: 2 (over x), tp: 8 (over z, y), section: 2 (over core).
Axes of the slice: x: 2, y: 2, z: 4, core: 2. Of those that a mesh axis runs over, the one named last changes fastest.
Arguments:
- hidden_in: bfloat16 [128, 4096], P(('grp', 'section')), parts along dimension 0, may hold values from -6 to 6
- temporal_gain: float32 [4096], replicated, may hold values from 0.5 to 1.5
- temporal_qkv: bfloat16 [3, 4096, 4096], P(None, None, 'tp'), may hold values from -0.09375 to 0.09375
- temporal_out_weight: bfloat16 [4096, 4096], P('tp'), may hold values from -0.125 to 0.125
- cache_keys: bfloat16 [128, 64, 4096], P(('grp', 'section'), None, 'tp'), parts along dimension 0, may hold values from -240 to 240
- cache_values: bfloat16 [128, 64, 4096], P(('grp', 'section'), None, 'tp'), parts along dimension 0, may hold values from -6 to 6
- lengths: int32 [128], P(('grp', 'section')), parts along dimension 0, may hold values from 1 to 64, as said below
- depth_in: bfloat16 [8, 4096, 1024], P('section', 'tp'), may hold values from -0.09375 to 0.09375
- depth_embed: bfloat16 [8, 2048, 1024], P('section', 'tp'), may hold values from -6 to 6
- depth_gain: float32 [1024], replicated, may hold values from 0.5 to 1.5
- depth_qkv: bfloat16 [8, 3, 1024, 1024], P('section', None, None, 'tp'), may hold values from -0.1875 to 0.1875
- depth_out_weight: bfloat16 [8, 1024, 1024], P('section', 'tp'), may hold values from -0.1875 to 0.1875
- head_gain: float32 [1024], replicated, may hold values from 0.5 to 1.5
- head_weight: bfloat16 [8, 1024, 2048], P('section', 'tp'), may hold values from -0.25 to 0.25
- tokens: int32 [128, 8], P('grp', 'section'), parts along dimension 0, may hold values from 0 to 2047
Outputs:
- temporal_out: bfloat16 [128, 4096], P(('grp', 'section'), 'tp'), parts along dimension 0
- logits: float32 [128, 8, 2048], P('grp', 'section', 'tp'), parts along dimension 0
The draws below stay inside these ranges and needn't reach their ends.
There are 2 independent parts, one for each index of `grp`. The reference program is written for one: setup_inputs(seed, part) draws one part's arguments, and reference() takes and returns one part's arrays. A program takes and returns all parts, laid end to end along the dimension named above; an argument that names none is the same for every part. Nothing has to cross between parts.
Inputs may be any that keep to these rules, and one draw needn't show every extreme that they name: Cached positions 0 to lengths - 1 of a stream are live and the new token stands at position lengths; some stream of every group holds 64 live positions.
All inputs are finite; a program needn't handle non-finite values.
Results may differ from the reference program's by a relative error of at most 0.009.
Values may be sent and summed in bfloat16 or wider, within the bound.
A program may use at most 64 MiB of HBM per device.

```python
import math
import jax
import jax.numpy as jnp
from jax import lax

D = 4096
HEADS = 32
HEAD_DIM = 128
DEPTH_D = 1024
DEPTH_HEADS = 16
DEPTH_HDIM = 64
VOCAB = 2048
CODEBOOKS = 8
STREAMS = 64
CACHE = 64


def draw_cache_keys(key, part):
    sample = jnp.clip(jax.random.normal(key, (STREAMS, CACHE, D), jnp.float32), -6.0, 6.0)
    return sample.astype(jnp.bfloat16)


def draw_lengths(key, part):
    drawn = jax.random.randint(key, (STREAMS,), 1, CACHE + 1, dtype=jnp.int32)
    where_full = jax.random.randint(jax.random.fold_in(key, 5), (), 0, STREAMS, dtype=jnp.int32)
    return drawn.at[where_full].set(CACHE)


def plant(entries, own_key, low, largest):
    dims = entries.shape
    spot = [jax.random.randint(jax.random.fold_in(own_key, axis), (), 0, dims[axis]) for axis in range(len(dims))]
    entries = entries.at[tuple(spot)].set(low)
    longest = dims.index(max(dims))
    spot[longest] = (spot[longest] + 1) % dims[longest]
    return entries.at[tuple(spot)].set(largest)


def raised(entries, key, source, target, parts, factor):
    owner, partner = [(jnp.arange(entries.shape[dim]) // (entries.shape[dim] // parts)).reshape([-1 if axis == dim else 1 for axis in range(entries.ndim)]) for dim in (source, target)]
    chosen = jax.random.permutation(key, parts)[partner]
    strong = (owner == chosen) | (owner == (partner + parts // 2) % parts)
    return jnp.where(strong, factor * entries, entries)


def steps_of(stream_key, shape, split, low, high):
    factor_of = 1.0
    for axis_at, blocks in split:
        heights = jax.random.uniform(jax.random.fold_in(jax.random.fold_in(stream_key, 6), axis_at), (blocks,), jnp.float32, low / len(split), high / len(split))
        factor_of = factor_of * jnp.repeat(jnp.exp(heights), shape[axis_at] // blocks).reshape((-1,) + (1,) * (len(shape) - 1 - axis_at))
    return factor_of


def normal_values(key, extent, scale, most, split=(), held_as=jnp.bfloat16):
    result = scale * jax.random.normal(key, extent, jnp.float32)
    if split:
        result = result * steps_of(key, extent, split, -0.22, 0.18)
    return jnp.clip(result, -most, most).astype(held_as)


def bell_draw_with(own_key, dims, width, reach, split, heavy, kind=jnp.bfloat16):
    result = width * jax.random.normal(own_key, dims, jnp.float32)
    if split:
        result = result * steps_of(own_key, dims, split, -0.22, 0.18)
    return jnp.clip(raised(result, jax.random.fold_in(own_key, 3), *heavy), -reach, reach).astype(kind)


def setup_inputs(seed: int = 0, part: int = 0) -> dict:
    streams_of = jax.random.split(jax.random.key(seed), 16)
    part_keys = jax.random.split(jax.random.fold_in(streams_of[15], part), 16)
    return {
        "hidden_in": normal_values(part_keys[0], (STREAMS, D), 1.0, 6.0, ((0, 2),)),
        "temporal_gain": jnp.clip(1.0 + 0.1 * jax.random.normal(streams_of[1], (D,), jnp.float32), 0.5, 1.5),
        "temporal_qkv": normal_values(streams_of[2], (3, D, D), D ** -0.5, 0.09375, ((2, 8),)),
        "temporal_out_weight": bell_draw_with(streams_of[3], (D, D), D ** -0.5, 0.125, ((0, 8),), (0, 1, 8, 2.0)),
        "cache_keys": draw_cache_keys(jax.random.fold_in(jax.random.fold_in(streams_of[15], part), 71), part),
        "cache_values": normal_values(part_keys[5], (STREAMS, CACHE, D), 1.0, 6.0, ((0, 2), (2, 8))),
        "lengths": draw_lengths(jax.random.fold_in(jax.random.fold_in(streams_of[15], part), 71), part),
        "depth_in": normal_values(streams_of[7], (CODEBOOKS, D, DEPTH_D), D ** -0.5, 0.09375, ((0, 2), (1, 8))),
        "depth_embed": normal_values(streams_of[8], (CODEBOOKS, VOCAB, DEPTH_D), 1.0, 6.0, ((0, 2), (1, 8))),
        "depth_gain": jnp.clip(1.0 + 0.1 * jax.random.normal(streams_of[9], (DEPTH_D,), jnp.float32), 0.5, 1.5),
        "depth_qkv": normal_values(streams_of[10], (CODEBOOKS, 3, DEPTH_D, DEPTH_D), DEPTH_D ** -0.5, 0.1875, ((0, 2), (3, 8))),
        "depth_out_weight": normal_values(streams_of[11], (CODEBOOKS, DEPTH_D, DEPTH_D), DEPTH_D ** -0.5, 0.1875, ((0, 2), (1, 8))),
        "head_gain": jnp.clip(1.0 + 0.1 * jax.random.normal(streams_of[12], (DEPTH_D,), jnp.float32), 0.5, 1.5),
        "head_weight": bell_draw_with(streams_of[13], (CODEBOOKS, DEPTH_D, VOCAB), DEPTH_D ** -0.5, 0.25, ((0, 2), (1, 8)), (1, 2, 8, 2.0)),
        "tokens": plant(jax.random.randint(part_keys[14], (STREAMS, CODEBOOKS), 0, VOCAB), jax.random.fold_in(part_keys[14], 1), 0, VOCAB - 1).astype(jnp.int32),
    }


EPSILON = 1e-05

def rms_norm(values, scale):
    wide = values.astype(jnp.float32)
    return wide * lax.rsqrt(lax.optimization_barrier(jnp.mean(wide * wide, axis=-1, keepdims=True)) + EPSILON) * scale.astype(jnp.float32)

def rotate(vectors, positions):
    halfdim = vectors.shape[-1] // 2
    spacing = jnp.arange(halfdim, dtype=jnp.float32) / halfdim
    inverse = jnp.exp(-math.log(10000.0) * spacing)
    angles = positions.astype(jnp.float32)[:, None, None] * inverse[None, None, :]
    cosine = jnp.cos(angles)
    sine = jnp.sin(angles)
    first = vectors[..., :halfdim]
    second = vectors[..., halfdim:]
    return jnp.concatenate([first * cosine - second * sine, first * sine + second * cosine], axis=-1)

def reference(hidden_in, temporal_gain, temporal_qkv, temporal_out_weight, cache_keys, cache_values, lengths, depth_in, depth_embed, depth_gain, depth_qkv, depth_out_weight, head_gain, head_weight, tokens):
    streams = hidden_in.shape[0]
    normed = rms_norm(hidden_in, temporal_gain).astype(jnp.bfloat16)
    projected = [jnp.dot(normed, temporal_qkv[number], preferred_element_type=jnp.float32) for number in range(3)]
    layout = (streams, HEADS, HEAD_DIM)
    queries = rotate(projected[0].reshape(layout), lengths).astype(jnp.bfloat16)
    keys_new = rotate(projected[1].reshape(layout), lengths).astype(jnp.bfloat16)
    values_new = projected[2].reshape(layout).astype(jnp.bfloat16)
    cached_keys = cache_keys.reshape(streams, CACHE, HEADS, HEAD_DIM).astype(jnp.float32)
    cached_values = cache_values.reshape(streams, CACHE, HEADS, HEAD_DIM).astype(jnp.float32)
    factor = 1.0 / math.sqrt(HEAD_DIM)
    scores = jnp.einsum('shd,sphd->shp', queries.astype(jnp.float32), cached_keys) * factor
    own_score = lax.optimization_barrier(jnp.sum(queries.astype(jnp.float32) * keys_new.astype(jnp.float32), axis=-1)) * factor
    valid = jnp.arange(CACHE, dtype=jnp.int32)[None, None, :] < lengths[:, None, None]
    scores = jnp.where(valid, scores, -jnp.inf)
    highest = jnp.maximum(lax.optimization_barrier(jnp.max(scores, axis=-1)), own_score)
    expo = jnp.exp(scores - highest[..., None])
    own_expo = jnp.exp(own_score - highest)
    totals = lax.optimization_barrier(jnp.sum(expo, axis=-1)) + own_expo
    weights = (expo / totals[..., None]).astype(jnp.bfloat16)
    own_weight = (own_expo / totals).astype(jnp.bfloat16)
    mixed = jnp.einsum('shp,sphd->shd', weights.astype(jnp.float32), cached_values)
    mixed = mixed + own_weight.astype(jnp.float32)[..., None] * values_new.astype(jnp.float32)
    mixed = mixed.astype(jnp.bfloat16).reshape(streams, D)
    temporal = (hidden_in.astype(jnp.float32) + jnp.dot(mixed, temporal_out_weight, preferred_element_type=jnp.float32)).astype(jnp.bfloat16)
    codes = depth_in.shape[0]
    entry = jnp.einsum('sd,cde->sce', temporal.astype(jnp.float32), depth_in.astype(jnp.float32))
    embedded = depth_embed[jnp.arange(codes, dtype=jnp.int32)[None, :], tokens]
    entry = entry + embedded.astype(jnp.float32)
    depth_normed = rms_norm(entry, depth_gain).astype(jnp.bfloat16)
    dproj = [jnp.einsum('sce,cef->scf', depth_normed.astype(jnp.float32), depth_qkv[:, number].astype(jnp.float32)).astype(jnp.bfloat16) for number in range(3)]
    shaped = [item.reshape(streams, codes, DEPTH_HEADS, DEPTH_HDIM).astype(jnp.float32) for item in dproj]
    depth_scores = jnp.einsum('sqhd,skhd->shqk', shaped[0], shaped[1]) * (1.0 / math.sqrt(DEPTH_HDIM))
    causal = jnp.arange(codes)[None, :] <= jnp.arange(codes)[:, None]
    depth_scores = jnp.where(causal[None, None], depth_scores, -jnp.inf)
    depth_top = lax.optimization_barrier(jnp.max(depth_scores, axis=-1, keepdims=True))
    depth_expo = jnp.exp(depth_scores - depth_top)
    depth_weights = (depth_expo / lax.optimization_barrier(jnp.sum(depth_expo, axis=-1, keepdims=True))).astype(jnp.bfloat16)
    depth_mixed = jnp.einsum('shqk,skhd->sqhd', depth_weights.astype(jnp.float32), shaped[2]).astype(jnp.bfloat16)
    depth_mixed = depth_mixed.reshape(streams, codes, DEPTH_D)
    resid = entry + jnp.einsum('scf,cfe->sce', depth_mixed.astype(jnp.float32), depth_out_weight.astype(jnp.float32))
    head_normed = rms_norm(resid, head_gain).astype(jnp.bfloat16)
    logits = jnp.einsum('sce,cev->scv', head_normed.astype(jnp.float32), head_weight.astype(jnp.float32))
    return (temporal, logits)
```

```python
import functools
import math

import jax
import jax.numpy as jnp
from jax import lax
from jax.experimental import pallas as pl
from jax.experimental.pallas import tpu as pltpu
from jax.sharding import PartitionSpec as P

HEAD_DIM = 128
DEPTH_HDIM = 64


EPSILON = 1e-05


def passed_along(block, axis, distance):
    devices = range(lax.axis_size(axis))
    route = [(i - distance, i) for i in devices if i - distance in devices]
    return lax.ppermute(block, axis, route)


def from_partner(shard, axis, distance):
    return lax.ppermute(shard, axis, [(i, i ^ 1 << distance) for i in range(lax.axis_size(axis))])


def rms_norm(values, scale):
    wide = values.astype(jnp.float32)
    return wide * lax.rsqrt(jnp.mean(wide * wide, axis=-1, keepdims=True) + EPSILON) * scale


def rotate(vectors, positions):
    halfdim = vectors.shape[-1] // 2
    spacing = jnp.arange(halfdim, dtype=jnp.float32) / halfdim
    inverse = jnp.exp(-math.log(10000.0) * spacing)
    angles = positions.astype(jnp.float32)[:, None, None] * inverse[None, None, :]
    cosine = jnp.cos(angles)
    sine = jnp.sin(angles)
    first = vectors[..., :halfdim]
    second = vectors[..., halfdim:]
    return jnp.concatenate(
        [first * cosine - second * sine, first * sine + second * cosine], axis=-1
    )


def per_device(
    hidden_in,
    temporal_gain,
    temporal_qkv,
    temporal_out_weight,
    cache_keys,
    cache_values,
    lengths,
    depth_in,
    depth_embed,
    depth_gain,
    depth_qkv,
    depth_out_weight,
    head_gain,
    head_weight,
    tokens,
):
    local_streams = hidden_in.shape[0]
    local_cols = temporal_qkv.shape[2]
    local_heads = local_cols // HEAD_DIM
    cache_len = cache_keys.shape[1]
    normed = rms_norm(hidden_in, temporal_gain).astype(jnp.bfloat16)
    projected = jnp.einsum("sd,tdf->tsf", normed, temporal_qkv, preferred_element_type=jnp.float32)
    layout = (local_streams, local_heads, HEAD_DIM)
    queries = rotate(projected[0].reshape(layout), lengths).astype(jnp.bfloat16)
    keys_new = rotate(projected[1].reshape(layout), lengths).astype(jnp.bfloat16)
    values_new = projected[2].reshape(layout).astype(jnp.bfloat16)
    cached_keys = cache_keys.reshape(local_streams, cache_len, local_heads, HEAD_DIM)
    cached_values = cache_values.reshape(local_streams, cache_len, local_heads, HEAD_DIM)
    factor = 1.0 / math.sqrt(HEAD_DIM)
    scores = (
        jnp.einsum("shd,sphd->shp", queries, cached_keys, preferred_element_type=jnp.float32)
        * factor
    )
    own_score = (
        jnp.sum(queries.astype(jnp.float32) * keys_new.astype(jnp.float32), axis=-1) * factor
    )
    valid = jnp.arange(cache_len, dtype=jnp.int32)[None, None, :] < lengths[:, None, None]
    scores = jnp.where(valid, scores, -jnp.inf)
    highest = jnp.maximum(jnp.max(scores, axis=-1), own_score)
    expo = jnp.exp(scores - highest[..., None])
    own_expo = jnp.exp(own_score - highest)
    totals = jnp.sum(expo, axis=-1) + own_expo
    weights = (expo / totals[..., None]).astype(jnp.bfloat16)
    own_weight = (own_expo / totals).astype(jnp.bfloat16)
    mixed = jnp.einsum("shp,sphd->shd", weights, cached_values, preferred_element_type=jnp.float32)
    mixed = mixed + own_weight.astype(jnp.float32)[..., None] * values_new.astype(jnp.float32)
    mixed = mixed.astype(jnp.bfloat16).reshape(local_streams, local_cols)
    partial_rows = jnp.dot(mixed, temporal_out_weight, preferred_element_type=jnp.float32)
    summed = lax.psum_scatter(partial_rows, "tp", scatter_dimension=1, tiled=True)
    slice_width = summed.shape[1]
    tp_place = lax.axis_index("tp")
    resid_in = lax.dynamic_slice_in_dim(hidden_in, tp_place * slice_width, slice_width, 1)
    temporal = (resid_in.astype(jnp.float32) + summed).astype(jnp.bfloat16)
    all_rows = lax.all_gather(temporal, "section", axis=0, tiled=True)
    streams = all_rows.shape[0]
    codes = depth_in.shape[0]
    entry_part = jnp.einsum("sd,cde->sce", all_rows, depth_in, preferred_element_type=jnp.float32)
    vocab_local = depth_embed.shape[1]
    first_id = tp_place * vocab_local
    onehot = (
        tokens[:, :, None] == first_id + jnp.arange(vocab_local, dtype=jnp.int32)[None, None, :]
    ).astype(jnp.bfloat16)
    embedded = jnp.einsum("scv,cve->sce", onehot, depth_embed, preferred_element_type=jnp.float32)
    entry_terms = entry_part + embedded
    hidden_rows = head_weight.shape[1]
    hidden_start = tp_place * hidden_rows
    entry = lax.psum(entry_terms, "tp")
    depth_normed = rms_norm(entry, depth_gain).astype(jnp.bfloat16)
    dproj = jnp.einsum(
        "sce,ctef->tscf", depth_normed, depth_qkv, preferred_element_type=jnp.float32
    ).astype(jnp.bfloat16)
    prior_keys, prior_values = passed_along((dproj[1], dproj[2]), "section", 1)
    depth_cols = dproj.shape[3]
    head_part = min(depth_cols, DEPTH_HDIM)
    local_parts = depth_cols // head_part
    sharers = DEPTH_HDIM // head_part
    all_keys = jnp.concatenate([prior_keys, dproj[1]], axis=1).reshape(
        streams, 2 * codes, local_parts, head_part
    )
    all_values = jnp.concatenate([prior_values, dproj[2]], axis=1).reshape(
        streams, 2 * codes, local_parts, head_part
    )
    depth_queries = dproj[0].reshape(streams, codes, local_parts, head_part)
    depth_scores = jnp.einsum(
        "sqhd,skhd->shqk", depth_queries, all_keys, preferred_element_type=jnp.float32
    )
    for level in range(sharers.bit_length() - 1):
        depth_scores = depth_scores + from_partner(depth_scores, "tp", level)
    depth_scores = depth_scores * (1.0 / math.sqrt(DEPTH_HDIM))
    section_place = lax.axis_index("section")
    query_pos = jnp.arange(codes, dtype=jnp.int32)[:, None]
    key_pos = jnp.arange(2 * codes, dtype=jnp.int32)[None, :]
    allowed = jnp.where(key_pos < codes, section_place > 0, key_pos - codes <= query_pos)
    depth_scores = jnp.where(allowed[None, None], depth_scores, -jnp.inf)
    depth_top = jnp.max(depth_scores, axis=-1, keepdims=True)
    depth_expo = jnp.exp(depth_scores - depth_top)
    depth_weights = (depth_expo / jnp.sum(depth_expo, axis=-1, keepdims=True)).astype(jnp.bfloat16)
    depth_mixed = jnp.einsum(
        "shqk,skhd->sqhd", depth_weights, all_values, preferred_element_type=jnp.float32
    ).astype(jnp.bfloat16)
    depth_mixed = depth_mixed.reshape(streams, codes, depth_cols)
    depth_terms = jnp.einsum(
        "scf,cfe->sce", depth_mixed, depth_out_weight, preferred_element_type=jnp.float32
    )
    resid = entry + lax.psum(depth_terms, "tp")
    head_normed = rms_norm(resid, head_gain).astype(jnp.bfloat16)
    own_hidden = lax.dynamic_slice_in_dim(head_normed, hidden_start, hidden_rows, 2)
    partial_logits = jnp.einsum(
        "sce,cev->scv", own_hidden, head_weight, preferred_element_type=jnp.float32
    )
    logits = lax.psum_scatter(partial_logits, "tp", scatter_dimension=2, tiled=True)
    return (temporal, logits)


MESH = pl.DeviceIdType.MESH


def normalised(wide, scale):
    return wide * lax.rsqrt(jnp.mean(wide * wide, axis=-1, keepdims=True) + EPSILON) * scale


def product(left, right):
    return jnp.dot(left, right, preferred_element_type=jnp.float32)


def tick_kernel(
    n, pieces,
    hidden_ref, gain_ref, lens_ref, tokens_ref, dgain_ref, hgain_ref,
    qkv_hbm, keys_hbm, values_hbm, outw_hbm, din_hbm, emb_hbm, dqkv_hbm, dout_hbm, headw_hbm,
    temporal_ref, logits_ref,
    qkv, keys, values, outw, din, emb, dqkv, dout, headw,
    tbuf, rows, ent, ebuf, nrm, kvs, kvr, mix, dbuf, lbuf, squares,
    load_sem, send_sem, recv_sem, pair_send, pair_recv,
):
    me = lax.axis_index("tp")
    sec = lax.axis_index("section")
    s_local, width = hidden_ref.shape
    cols = qkv.shape[2]
    heads = cols // HEAD_DIM
    cache_len = keys.shape[1]
    codes = din.shape[0]
    streams = 2 * s_local
    bf = jnp.bfloat16

    span = width // pieces
    loads = {}
    slot = 0

    def load(name, source, target):
        nonlocal slot
        loads[name] = pltpu.make_async_copy(source, target, load_sem.at[slot])
        loads[name].start()
        slot += 1

    for t in range(3):
        for k in range(pieces):
            part = pl.ds(k * span, span)
            load(("qkv", t, k), qkv_hbm.at[t, part, :], qkv.at[t, part, :])
    load("keys", keys_hbm, keys)
    load("values", values_hbm, values)
    load("outw", outw_hbm, outw)
    barrier = pltpu.get_barrier_semaphore()
    for d in range(1, n):
        pl.semaphore_signal(
            barrier, inc=1, device_id={"tp": lax.rem(me + d, n)}, device_id_type=MESH
        )
    pl.semaphore_signal(barrier, inc=1, device_id={"section": 1 - sec}, device_id_type=MESH)

    def to_peer(phase, d, source, target, peer):
        return pltpu.make_async_remote_copy(
            src_ref=source, dst_ref=target,
            send_sem=send_sem.at[phase, d], recv_sem=recv_sem.at[phase, d],
            device_id={"tp": peer}, device_id_type=MESH,
        )

    def to_partner(phase, source, target):
        return pltpu.make_async_remote_copy(
            src_ref=source, dst_ref=target,
            send_sem=pair_send.at[phase], recv_sem=pair_recv.at[phase],
            device_id={"section": 1 - sec}, device_id_type=MESH,
        )

    pending = []
    half_n = n // 2
    pair = lax.rem(me, 2)
    spot = me // 2
    mate = 2 * spot + 1 - pair
    order = sorted(range(1, half_n), key=lambda d: abs(d - half_n // 2))

    def halves(size):
        return [(h, slice(h * size // 2, (h + 1) * size // 2)) for h in range(2)]

    def summed_over_tp(phase, block_of, buf):
        firsts = []
        parts = halves(buf.shape[2])
        for i, d in enumerate(order + [0]):
            target = lax.rem(spot + d, half_n)
            buf[0, i] = block_of(2 * target + 1 - pair).astype(bf)
            for h, at in parts:
                firsts.append(
                    to_peer(2 * phase, 2 * i + h, buf.at[0, i, at], buf.at[1, i, at], mate)
                )
                firsts[-1].start()
        seconds = []
        for i, d in enumerate(order + [0]):
            target = lax.rem(spot + d, half_n)
            block = block_of(2 * target + pair)
            added = []
            for h, at in parts:
                firsts[2 * i + h].wait_recv()
                added.append(block[at] + buf[1, i, at].astype(jnp.float32))
                if d:
                    buf[2, i, at] = added[-1].astype(bf)
                    seconds.append(
                        to_peer(
                            2 * phase + 1, 2 * i + h, buf.at[2, i, at], buf.at[3, i, at],
                            2 * target + pair,
                        )
                    )
                    seconds[-1].start()
        pending.extend(firsts + seconds)
        return jnp.concatenate(added, axis=0), seconds

    def finished(block, seconds, buf):
        for i in range(half_n - 1):
            seconds[2 * i].wait_recv()
            seconds[2 * i + 1].wait_recv()
            block = block + buf[3, i].astype(jnp.float32)
        return block

    normed = normalised(hidden_ref[...].astype(jnp.float32), gain_ref[...]).astype(bf)
    half = HEAD_DIM // 2
    lane = lax.broadcasted_iota(jnp.int32, (s_local, HEAD_DIM), 1)
    spacing = lax.rem(lane, half).astype(jnp.float32) / half
    diagonal = lax.broadcasted_iota(jnp.int32, (s_local, s_local), 0) == lax.broadcasted_iota(
        jnp.int32, (s_local, s_local), 1
    )
    lens = jnp.sum(
        jnp.where(diagonal, lens_ref[...].astype(jnp.float32), 0.0), axis=1, keepdims=True
    )
    lens = jnp.broadcast_to(lens, (s_local, HEAD_DIM))
    angles = lens * jnp.exp(-math.log(10000.0) * spacing)
    cosine = jnp.cos(angles)
    sine = jnp.sin(angles)
    sine = jnp.where(lane < half, -sine, sine)
    proj = []
    for t in range(3):
        acc = None
        for k in range(pieces):
            loads["qkv", t, k].wait()
            term = product(normed[:, k * span:(k + 1) * span], qkv[t, k * span:(k + 1) * span, :])
            acc = term if acc is None else acc + term
        if t == 1:
            load("emb", emb_hbm, emb)
            load("din", din_hbm, din)
            load("dqkv", dqkv_hbm, dqkv)
            load("dout", dout_hbm, dout)
            load("headw", headw_hbm, headw)
        if t < 2:
            turned = []
            for h in range(heads):
                one = acc[:, h * HEAD_DIM:(h + 1) * HEAD_DIM]
                turned.append(one * cosine + pltpu.roll(one, half, 1) * sine)
            acc = jnp.concatenate(turned, axis=1)
        proj.append(acc.astype(bf).astype(jnp.float32))

    factor = 1.0 / math.sqrt(HEAD_DIM)
    loads["keys"].wait()
    loads["values"].wait()
    group = 8
    padded = 8
    owner = lax.broadcasted_iota(jnp.int32, (group, padded, cols), 2) // HEAD_DIM
    mine = owner == lax.broadcasted_iota(jnp.int32, (group, padded, cols), 1)
    place = lax.broadcasted_iota(jnp.int32, (group, padded, cache_len), 2).astype(jnp.float32)
    mixed = []
    for g in range(s_local // group):
        at = slice(g * group, (g + 1) * group)
        q_g = jnp.where(mine, proj[0][at][:, None, :], 0.0)
        scores = lax.dot_general(
            q_g.astype(bf), keys[at], (((2,), (2,)), ((0,), (0,))),
            preferred_element_type=jnp.float32,
        ) * factor
        own_score = jnp.sum(q_g * proj[1][at][:, None, :], axis=-1, keepdims=True) * factor
        live = place < lens[at, :cache_len][:, None, :]
        scores = jnp.where(live, scores, -jnp.inf)
        highest = jnp.maximum(jnp.max(scores, axis=-1, keepdims=True), own_score)
        expo = jnp.exp(scores - highest)
        own_expo = jnp.exp(own_score - highest)
        totals = jnp.sum(expo, axis=-1, keepdims=True) + own_expo
        weights = (expo / totals).astype(bf)
        own_weight = (own_expo / totals).astype(bf).astype(jnp.float32)
        out = lax.dot_general(
            weights, values[at], (((2,), (1,)), ((0,), (0,))),
            preferred_element_type=jnp.float32,
        )
        out = jnp.where(mine, out + own_weight * proj[2][at][:, None, :], 0.0)
        mixed.append(jnp.sum(out, axis=1))
    mixed = jnp.concatenate(mixed, axis=0).astype(bf)

    loads["outw"].wait()
    slim = width // n
    pl.semaphore_wait(barrier, n)

    def row_block(j):
        return product(mixed, outw[:, pl.ds(pl.multiple_of(j * slim, slim), slim)])

    summed, seconds = summed_over_tp(0, row_block, tbuf)

    vocab = emb.shape[1]
    chunk_rows = codes * s_local
    loads["emb"].wait()
    ids = lax.broadcasted_iota(jnp.int32, (vocab, streams), 0) + me * vocab
    for c in range(codes):
        onehot = jnp.where(tokens_ref[c:c + 1, :] == ids, 1.0, 0.0).astype(bf)
        looked_up = lax.dot_general(
            onehot, emb[c], (((0,), (0,)), ((), ())), preferred_element_type=jnp.float32
        )
        for a in range(2):
            ent[a, c * s_local:(c + 1) * s_local, :] = looked_up[a * s_local:(a + 1) * s_local]
    loads["din"].wait()

    summed = finished(summed, seconds, tbuf)
    start = pl.multiple_of(me * slim, slim)
    temporal = (hidden_ref[:, pl.ds(start, slim)].astype(jnp.float32) + summed).astype(bf)
    temporal_ref[...] = temporal
    rows[sec] = temporal
    swap = to_partner(0, rows.at[sec], rows.at[sec])
    swap.start()
    pending.append(swap)
    swap.wait_recv()

    part = din.shape[2] // n
    share = headw.shape[2] // n
    lanes = dqkv.shape[3]

    def at_code(c):
        return slice(c * s_local, (c + 1) * s_local)

    def features(j):
        return pl.ds(pl.multiple_of(j * part, part), part)

    def first_sends(phase, a, block_of, buf):
        sent = []
        for i, d in enumerate(order + [0]):
            target = lax.rem(spot + d, half_n)
            buf[0, a, i] = block_of(2 * target + 1 - pair).astype(bf)
            sent.append(
                to_peer(2 * phase, 2 * i + a, buf.at[0, a, i], buf.at[1, a, i], mate)
            )
            sent[-1].start()
        pending.extend(sent)
        return sent

    def second_sends(phase, a, block_of, buf, firsts):
        sent = []
        for i, d in enumerate(order + [0]):
            target = lax.rem(spot + d, half_n)
            block = block_of(2 * target + pair)
            firsts[i].wait_recv()
            block = block + buf[1, a, i].astype(jnp.float32)
            if d:
                buf[2, a, i] = block.astype(bf)
                sent.append(
                    to_peer(
                        2 * phase + 1, 2 * i + a, buf.at[2, a, i], buf.at[3, a, i],
                        2 * target + pair,
                    )
                )
                sent[-1].start()
        pending.extend(sent)
        return block, sent

    def gathered(a, block, sent, buf):
        for i in range(half_n - 1):
            sent[i].wait_recv()
            block = block + buf[3, a, i].astype(jnp.float32)
        return block

    def entry_block(a):
        def block_of(j):
            terms = [product(rows[a], din[c, :, features(j)]) for c in range(codes)]
            return ent[a, :, features(j)] + jnp.concatenate(terms, axis=0)
        return block_of

    def row_squares(block):
        return lax.dot_general(
            jnp.ones((8, part), jnp.float32), block * block, (((1,), (1,)), ((), ())),
            preferred_element_type=jnp.float32, precision=lax.Precision.HIGHEST,
        )

    def squares_out(which, a, block):
        squares[which, a, me] = row_squares(block)
        sent = []
        for d in range(1, n):
            sent.append(
                to_peer(
                    8 + which + 4 * a, d, squares.at[which, a, me], squares.at[which, a, me],
                    lax.rem(me + d, n),
                )
            )
            sent[-1].start()
        pending.extend(sent)
        return sent

    def row_factor(which, a, sent):
        for copy in sent:
            copy.wait_recv()
        mean = jnp.sum(squares[which, a], axis=0) / (n * part)
        column = lax.dot_general(
            mean, jnp.full((8, 128), 0.125, jnp.float32), (((0,), (0,)), ((), ())),
            preferred_element_type=jnp.float32, precision=lax.Precision.HIGHEST,
        )
        return lax.rsqrt(column + EPSILON)

    def gather_sends(a, block):
        nrm[me, a] = (block * dgain_ref[:, features(me)]).astype(bf)
        copies = []
        for i, d in enumerate(order):
            peer = 2 * lax.rem(spot + d, half_n) + pair
            copies.append(to_peer(6, 2 * i + a, nrm.at[me, a], nrm.at[me, a], peer))
            copies[-1].start()
        swaps = [to_peer(6, n - 2 + a, nrm.at[me, a], nrm.at[me, a], mate)]
        swaps[0].start()
        return copies, swaps

    def gather_forwards(a, copies, swaps):
        for i, d in enumerate(order):
            came = 2 * lax.rem(spot - d + half_n, half_n) + pair
            copies[i].wait_recv()
            swaps.append(to_peer(7, 2 * i + a, nrm.at[came, a], nrm.at[came, a], mate))
            swaps[-1].start()
        pending.extend(copies + swaps)

    def projections(a, swaps, sent):
        r = row_factor(0, a, sent)
        for copy in swaps:
            copy.wait_recv()
        queries = []
        for c in range(codes):
            x = jnp.concatenate([nrm[j, a, at_code(c), :] for j in range(n)], axis=1)
            f = r[at_code(c)]
            queries.append((product(x, dqkv[c, 0]) * f).astype(bf).astype(jnp.float32))
            kvs[a, 0, c] = (product(x, dqkv[c, 1]) * f).astype(bf)
            kvs[a, 1, c] = (product(x, dqkv[c, 2]) * f).astype(bf)
        swap = to_partner(1 + a, kvs.at[a], kvr.at[a])
        swap.start()
        pending.append(swap)
        return queries, swap

    row_head = lax.rem(lax.broadcasted_iota(jnp.int32, (2 * lanes, lanes), 0), lanes) // DEPTH_HDIM
    col_head = lax.broadcasted_iota(jnp.int32, (2 * lanes, lanes), 1) // DEPTH_HDIM
    ones = jnp.where(row_head == col_head, 1.0, 0.0).astype(bf)
    scale = 1.0 / math.sqrt(DEPTH_HDIM)

    def score(query, key):
        both = query * key.astype(jnp.float32)
        high = both.astype(bf)
        low = (both - high.astype(jnp.float32)).astype(bf)
        return product(jnp.concatenate([high, low], axis=1), ones) * scale

    def attention(a, queries, swap):
        local = [[score(queries[q], kvs[a, 0, k]) for k in range(q + 1)] for q in range(codes)]
        swap.wait_recv()
        for q in range(codes):
            prior = [
                jnp.where(sec > 0, score(queries[q], kvr[a, 0, k]), -jnp.inf)
                for k in range(codes)
            ]
            every = prior + local[q]
            top = every[0]
            for item in every[1:]:
                top = jnp.maximum(top, item)
            expo = [jnp.exp(item - top) for item in every]
            sums = expo[0]
            for item in expo[1:]:
                sums = sums + item
            out = None
            for k, item in enumerate(expo):
                value = kvr[a, 1, k] if k < codes else kvs[a, 1, k - codes]
                term = (item / sums).astype(bf).astype(jnp.float32) * value.astype(jnp.float32)
                out = term if out is None else out + term
            mix[a, at_code(q), :] = out.astype(bf)

    def resid_block(a):
        def block_of(j):
            return jnp.concatenate(
                [product(mix[a, at_code(c), :], dout[c, :, features(j)]) for c in range(codes)],
                axis=0,
            )
        return block_of

    def vocab_block(hidden):
        def block_of(j):
            there = pl.ds(pl.multiple_of(j * share, share), share)
            return jnp.concatenate(
                [product(hidden[at_code(c), :], headw[c, :, there]) for c in range(codes)],
                axis=0,
            )
        return block_of

    both = range(2)
    blocks = [entry_block(a) for a in both]
    firsts = [first_sends(1, a, blocks[a], ebuf) for a in both]
    sums = [second_sends(1, a, blocks[a], ebuf, firsts[a]) for a in both]
    entry, square_sends, gathers = [], [], []
    for a in both:
        entry.append(gathered(a, *sums[a], ebuf))
        gathers.append(gather_sends(a, entry[a]))
        square_sends.append(squares_out(0, a, entry[a]))
    for a in both:
        gather_forwards(a, *gathers[a])
    loads["dqkv"].wait()
    loads["dout"].wait()
    blocks = [resid_block(a) for a in both]
    firsts = []
    for a in both:
        queries, swap = projections(a, gathers[a][1], square_sends[a])
        attention(a, queries, swap)
        firsts.append(first_sends(2, a, blocks[a], dbuf))
    sums = [second_sends(2, a, blocks[a], dbuf, firsts[a]) for a in both]
    loads["headw"].wait()
    square_sends, firsts, blocks = [], [], []
    for a in both:
        resid = entry[a] + gathered(a, *sums[a], dbuf)
        hidden = (resid * hgain_ref[:, features(me)]).astype(bf)
        blocks.append(vocab_block(hidden))
        firsts.append(first_sends(5, a, blocks[a], lbuf))
        square_sends.append(squares_out(1, a, resid))
    sums = [second_sends(5, a, blocks[a], lbuf, firsts[a]) for a in both]
    for a in both:
        out = gathered(a, *sums[a], lbuf) * row_factor(1, a, square_sends[a])[:, :1]
        logits_ref[:, a * s_local:(a + 1) * s_local, :] = out.reshape(codes, s_local, share)
    for copy in pending:
        copy.wait_send()


def fused(
    n, hidden_in, temporal_gain, temporal_qkv, temporal_out_weight, cache_keys, cache_values,
    lengths, depth_in, depth_embed, depth_gain, depth_qkv, depth_out_weight, head_gain,
    head_weight, tokens,
):
    s_local, width = hidden_in.shape
    codes, slim, deep = depth_in.shape
    streams = 2 * s_local
    total = codes * streams
    lanes = depth_qkv.shape[3]
    part = head_weight.shape[1]
    share = head_weight.shape[2] // n
    bf, f32 = jnp.bfloat16, jnp.float32
    pieces = 4
    big = [temporal_qkv, cache_keys, cache_values, temporal_out_weight, depth_in, depth_embed,
           depth_qkv, depth_out_weight, head_weight]
    vmem = pl.BlockSpec(memory_space=pltpu.VMEM)
    scratch = [pltpu.VMEM(a.shape, a.dtype) for a in big] + [
        pltpu.VMEM((4, n // 2, s_local, slim), bf),
        pltpu.VMEM((2, s_local, slim), bf),
        pltpu.VMEM((2, total // 2, deep), f32),
        pltpu.VMEM((4, 2, n // 2, total // 2, part), bf),
        pltpu.VMEM((n, 2, total // 2, part), bf),
        pltpu.VMEM((2, 2, codes, s_local, lanes), bf),
        pltpu.VMEM((2, 2, codes, s_local, lanes), bf),
        pltpu.VMEM((2, total // 2, lanes), bf),
        pltpu.VMEM((4, 2, n // 2, total // 2, part), bf),
        pltpu.VMEM((4, 2, n // 2, total // 2, share), bf),
        pltpu.VMEM((2, 2, n, 8, total // 2), f32),
        pltpu.SemaphoreType.DMA((3 * pieces + 8,)),
        pltpu.SemaphoreType.DMA((14, n)),
        pltpu.SemaphoreType.DMA((14, n)),
        pltpu.SemaphoreType.DMA((3,)),
        pltpu.SemaphoreType.DMA((3,)),
    ]
    temporal, logits = pl.pallas_call(
        functools.partial(tick_kernel, n, pieces),
        out_shape=(
            jax.ShapeDtypeStruct((s_local, slim), bf),
            jax.ShapeDtypeStruct((codes, streams, share), f32),
        ),
        in_specs=[vmem] * 6 + [pl.BlockSpec(memory_space=pl.ANY)] * 9,
        out_specs=(vmem, vmem),
        scratch_shapes=scratch,
        compiler_params=pltpu.CompilerParams(
            collective_id=0, has_side_effects=True, vmem_limit_bytes=60 * 1024 * 1024
        ),
    )(
        hidden_in, temporal_gain[None, :], lengths[None, :], tokens.T, depth_gain[None, :], head_gain[None, :],
        *big,
    )
    return temporal, jnp.swapaxes(logits, 0, 1)


def fits(n, arrays):
    hidden_in, depth_in, depth_qkv = arrays[0], arrays[7], arrays[10]
    total = depth_in.shape[0] * 2 * hidden_in.shape[0]
    return (
        lax.axis_size("section") == 2
        and n % 2 == 0
        and depth_qkv.shape[3] == 128
        and arrays[13].shape[1] % 128 == 0
        and arrays[13].shape[2] % (128 * n) == 0
        and total % 256 == 0
        and hidden_in.shape[0] % 16 == 0
        and arrays[4].shape[1] <= HEAD_DIM
        and arrays[2].shape[2] <= 8 * HEAD_DIM
    )


def any_size(*arrays):
    n = lax.axis_size("tp")
    if fits(n, arrays):
        return fused(n, *arrays)
    return per_device(*arrays)


def solution(mesh):
    return jax.shard_map(
        any_size,
        mesh=mesh,
        in_specs=(
            P(("grp", "section"), None),
            P(),
            P(None, None, "tp"),
            P("tp", None),
            P(("grp", "section"), None, "tp"),
            P(("grp", "section"), None, "tp"),
            P(("grp", "section")),
            P("section", "tp", None),
            P("section", "tp", None),
            P(),
            P("section", None, None, "tp"),
            P("section", "tp", None),
            P(),
            P("section", "tp", None),
            P("grp", "section"),
        ),
        out_specs=(P(("grp", "section"), "tp"), P("grp", "section", "tp")),
        check_vma=False,
    )
```

```python
import functools
import math

import jax
import jax.numpy as jnp
from jax import lax
from jax.experimental import pallas as pl
from jax.experimental.pallas import tpu as pltpu
from jax.sharding import PartitionSpec as P

HEAD_DIM = 128
DEPTH_HDIM = 64


EPSILON = 1e-05


def passed_along(block, axis, distance):
    devices = range(lax.axis_size(axis))
    route = [(i - distance, i) for i in devices if i - distance in devices]
    return lax.ppermute(block, axis, route)


def from_partner(shard, axis, distance):
    return lax.ppermute(shard, axis, [(i, i ^ 1 << distance) for i in range(lax.axis_size(axis))])


def rms_norm(values, scale):
    wide = values.astype(jnp.float32)
    return wide * lax.rsqrt(jnp.mean(wide * wide, axis=-1, keepdims=True) + EPSILON) * scale


def rotate(vectors, positions):
    halfdim = vectors.shape[-1] // 2
    spacing = jnp.arange(halfdim, dtype=jnp.float32) / halfdim
    inverse = jnp.exp(-math.log(10000.0) * spacing)
    angles = positions.astype(jnp.float32)[:, None, None] * inverse[None, None, :]
    cosine = jnp.cos(angles)
    sine = jnp.sin(angles)
    first = vectors[..., :halfdim]
    second = vectors[..., halfdim:]
    return jnp.concatenate(
        [first * cosine - second * sine, first * sine + second * cosine], axis=-1
    )


def per_device(
    hidden_in,
    temporal_gain,
    temporal_qkv,
    temporal_out_weight,
    cache_keys,
    cache_values,
    lengths,
    depth_in,
    depth_embed,
    depth_gain,
    depth_qkv,
    depth_out_weight,
    head_gain,
    head_weight,
    tokens,
):
    local_streams = hidden_in.shape[0]
    local_cols = temporal_qkv.shape[2]
    local_heads = local_cols // HEAD_DIM
    cache_len = cache_keys.shape[1]
    normed = rms_norm(hidden_in, temporal_gain).astype(jnp.bfloat16)
    projected = jnp.einsum("sd,tdf->tsf", normed, temporal_qkv, preferred_element_type=jnp.float32)
    layout = (local_streams, local_heads, HEAD_DIM)
    queries = rotate(projected[0].reshape(layout), lengths).astype(jnp.bfloat16)
    keys_new = rotate(projected[1].reshape(layout), lengths).astype(jnp.bfloat16)
    values_new = projected[2].reshape(layout).astype(jnp.bfloat16)
    cached_keys = cache_keys.reshape(local_streams, cache_len, local_heads, HEAD_DIM)
    cached_values = cache_values.reshape(local_streams, cache_len, local_heads, HEAD_DIM)
    factor = 1.0 / math.sqrt(HEAD_DIM)
    scores = (
        jnp.einsum("shd,sphd->shp", queries, cached_keys, preferred_element_type=jnp.float32)
        * factor
    )
    own_score = (
        jnp.sum(queries.astype(jnp.float32) * keys_new.astype(jnp.float32), axis=-1) * factor
    )
    valid = jnp.arange(cache_len, dtype=jnp.int32)[None, None, :] < lengths[:, None, None]
    scores = jnp.where(valid, scores, -jnp.inf)
    highest = jnp.maximum(jnp.max(scores, axis=-1), own_score)
    expo = jnp.exp(scores - highest[..., None])
    own_expo = jnp.exp(own_score - highest)
    totals = jnp.sum(expo, axis=-1) + own_expo
    weights = (expo / totals[..., None]).astype(jnp.bfloat16)
    own_weight = (own_expo / totals).astype(jnp.bfloat16)
    mixed = jnp.einsum("shp,sphd->shd", weights, cached_values, preferred_element_type=jnp.float32)
    mixed = mixed + own_weight.astype(jnp.float32)[..., None] * values_new.astype(jnp.float32)
    mixed = mixed.astype(jnp.bfloat16).reshape(local_streams, local_cols)
    partial_rows = jnp.dot(mixed, temporal_out_weight, preferred_element_type=jnp.float32)
    summed = lax.psum_scatter(partial_rows, "tp", scatter_dimension=1, tiled=True)
    slice_width = summed.shape[1]
    tp_place = lax.axis_index("tp")
    resid_in = lax.dynamic_slice_in_dim(hidden_in, tp_place * slice_width, slice_width, 1)
    temporal = (resid_in.astype(jnp.float32) + summed).astype(jnp.bfloat16)
    all_rows = lax.all_gather(temporal, "section", axis=0, tiled=True)
    streams = all_rows.shape[0]
    codes = depth_in.shape[0]
    entry_part = jnp.einsum("sd,cde->sce", all_rows, depth_in, preferred_element_type=jnp.float32)
    vocab_local = depth_embed.shape[1]
    first_id = tp_place * vocab_local
    onehot = (
        tokens[:, :, None] == first_id + jnp.arange(vocab_local, dtype=jnp.int32)[None, None, :]
    ).astype(jnp.bfloat16)
    embedded = jnp.einsum("scv,cve->sce", onehot, depth_embed, preferred_element_type=jnp.float32)
    entry_terms = entry_part + embedded
    hidden_rows = head_weight.shape[1]
    hidden_start = tp_place * hidden_rows
    entry = lax.psum(entry_terms, "tp")
    depth_normed = rms_norm(entry, depth_gain).astype(jnp.bfloat16)
    dproj = jnp.einsum(
        "sce,ctef->tscf", depth_normed, depth_qkv, preferred_element_type=jnp.float32
    ).astype(jnp.bfloat16)
    prior_keys, prior_values = passed_along((dproj[1], dproj[2]), "section", 1)
    depth_cols = dproj.shape[3]
    head_part = min(depth_cols, DEPTH_HDIM)
    local_parts = depth_cols // head_part
    sharers = DEPTH_HDIM // head_part
    all_keys = jnp.concatenate([prior_keys, dproj[1]], axis=1).reshape(
        streams, 2 * codes, local_parts, head_part
    )
    all_values = jnp.concatenate([prior_values, dproj[2]], axis=1).reshape(
        streams, 2 * codes, local_parts, head_part
    )
    depth_queries = dproj[0].reshape(streams, codes, local_parts, head_part)
    depth_scores = jnp.einsum(
        "sqhd,skhd->shqk", depth_queries, all_keys, preferred_element_type=jnp.float32
    )
    for level in range(sharers.bit_length() - 1):
        depth_scores = depth_scores + from_partner(depth_scores, "tp", level)
    depth_scores = depth_scores * (1.0 / math.sqrt(DEPTH_HDIM))
    section_place = lax.axis_index("section")
    query_pos = jnp.arange(codes, dtype=jnp.int32)[:, None]
    key_pos = jnp.arange(2 * codes, dtype=jnp.int32)[None, :]
    allowed = jnp.where(key_pos < codes, section_place > 0, key_pos - codes <= query_pos)
    depth_scores = jnp.where(allowed[None, None], depth_scores, -jnp.inf)
    depth_top = jnp.max(depth_scores, axis=-1, keepdims=True)
    depth_expo = jnp.exp(depth_scores - depth_top)
    depth_weights = (depth_expo / jnp.sum(depth_expo, axis=-1, keepdims=True)).astype(jnp.bfloat16)
    depth_mixed = jnp.einsum(
        "shqk,skhd->sqhd", depth_weights, all_values, preferred_element_type=jnp.float32
    ).astype(jnp.bfloat16)
    depth_mixed = depth_mixed.reshape(streams, codes, depth_cols)
    depth_terms = jnp.einsum(
        "scf,cfe->sce", depth_mixed, depth_out_weight, preferred_element_type=jnp.float32
    )
    resid = entry + lax.psum(depth_terms, "tp")
    head_normed = rms_norm(resid, head_gain).astype(jnp.bfloat16)
    own_hidden = lax.dynamic_slice_in_dim(head_normed, hidden_start, hidden_rows, 2)
    partial_logits = jnp.einsum(
        "sce,cev->scv", own_hidden, head_weight, preferred_element_type=jnp.float32
    )
    logits = lax.psum_scatter(partial_logits, "tp", scatter_dimension=2, tiled=True)
    return (temporal, logits)


MESH = pl.DeviceIdType.MESH


def normalised(wide, scale):
    return wide * lax.rsqrt(jnp.mean(wide * wide, axis=-1, keepdims=True) + EPSILON) * scale


def product(left, right):
    return jnp.dot(left, right, preferred_element_type=jnp.float32)


def tick_kernel(
    n, pieces,
    hidden_ref, gain_ref, lens_ref, tokens_ref, dgain_ref, hgain_ref,
    qkv_hbm, keys_hbm, values_hbm, outw_hbm, din_hbm, emb_hbm, dqkv_hbm, dout_hbm, headw_hbm,
    temporal_ref, logits_ref,
    qkv, keys, values, outw, din, emb, dqkv, dout, headw,
    tbuf, rows, ent, ebuf, nrm, kvs, kvr, mix, dbuf, lbuf, squares, qs, entry,
    load_sem, send_sem, recv_sem, pair_send, pair_recv,
):
    me = lax.axis_index("tp")
    sec = lax.axis_index("section")
    s_local, width = hidden_ref.shape
    cols = qkv.shape[2]
    heads = cols // HEAD_DIM
    cache_len = keys.shape[1]
    codes = din.shape[0]
    streams = 2 * s_local
    bf = jnp.bfloat16

    span = width // pieces
    loads = {}
    slot = 0

    def load(name, source, target):
        nonlocal slot
        loads[name] = pltpu.make_async_copy(source, target, load_sem.at[slot])
        loads[name].start()
        slot += 1

    for t in range(3):
        for k in range(pieces):
            part = pl.ds(k * span, span)
            load(("qkv", t, k), qkv_hbm.at[t, part, :], qkv.at[t, part, :])
    load("keys", keys_hbm, keys)
    load("values", values_hbm, values)
    load("outw", outw_hbm, outw)
    barrier = pltpu.get_barrier_semaphore()
    for d in range(1, n):
        pl.semaphore_signal(
            barrier, inc=1, device_id={"tp": lax.rem(me + d, n)}, device_id_type=MESH
        )
    pl.semaphore_signal(barrier, inc=1, device_id={"section": 1 - sec}, device_id_type=MESH)

    arrivals = {}

    def arrival(phase, d):
        if phase == 10:
            phase = 2
        return arrivals.setdefault((phase, d), len(arrivals))

    def to_peer(phase, d, source, target, peer):
        return pltpu.make_async_remote_copy(
            src_ref=source, dst_ref=target,
            send_sem=send_sem.at[phase], recv_sem=recv_sem.at[arrival(phase, d)],
            device_id={"tp": peer}, device_id_type=MESH,
        )

    def all_came(phase, d, there):
        to_peer(phase, d, there, there, mate).wait_recv()

    def all_sent(phase, sent):
        to_peer(phase, 0, sent, sent, mate).wait_send()

    def to_partner(phase, source, target):
        return pltpu.make_async_remote_copy(
            src_ref=source, dst_ref=target,
            send_sem=pair_send.at[phase], recv_sem=pair_recv.at[phase],
            device_id={"section": 1 - sec}, device_id_type=MESH,
        )

    half_n = n // 2
    pair = lax.rem(me, 2)
    spot = me // 2
    mate = 2 * spot + 1 - pair
    order = sorted(range(1, half_n), key=lambda d: abs(d - half_n // 2))

    def halves(size):
        return [(h, slice(h * size // 2, (h + 1) * size // 2)) for h in range(2)]

    def summed_over_tp(phase, block_of, buf):
        firsts = []
        parts = halves(buf.shape[2])
        for i, d in enumerate(order + [0]):
            target = lax.rem(spot + d, half_n)
            buf[0, i] = block_of(2 * target + 1 - pair).astype(bf)
            for h, at in parts:
                firsts.append(
                    to_peer(2 * phase, 2 * i + h, buf.at[0, i, at], buf.at[1, i, at], mate)
                )
                firsts[-1].start()
        for i, d in enumerate(order + [0]):
            target = lax.rem(spot + d, half_n)
            block = block_of(2 * target + pair)
            added = []
            for h, at in parts:
                firsts[2 * i + h].wait_recv()
                added.append(block[at] + buf[1, i, at].astype(jnp.float32))
                if d:
                    buf[2, i, at] = added[-1].astype(bf)
                    to_peer(
                        2 * phase + 1, 0, buf.at[2, i, at], buf.at[3, i, at], 2 * target + pair
                    ).start()
        return jnp.concatenate(added, axis=0)

    def finished(phase, block, buf):
        all_came(2 * phase + 1, 0, buf.at[3, pl.ds(0, half_n - 1)])
        for i in range(half_n - 1):
            block = block + buf[3, i].astype(jnp.float32)
        return block

    normed = normalised(hidden_ref[...].astype(jnp.float32), gain_ref[...]).astype(bf)
    half = HEAD_DIM // 2
    lane = lax.broadcasted_iota(jnp.int32, (s_local, HEAD_DIM), 1)
    spacing = lax.rem(lane, half).astype(jnp.float32) / half
    diagonal = lax.broadcasted_iota(jnp.int32, (s_local, s_local), 0) == lax.broadcasted_iota(
        jnp.int32, (s_local, s_local), 1
    )
    lens = jnp.sum(
        jnp.where(diagonal, lens_ref[...].astype(jnp.float32), 0.0), axis=1, keepdims=True
    )
    lens = jnp.broadcast_to(lens, (s_local, HEAD_DIM))
    angles = lens * jnp.exp(-math.log(10000.0) * spacing)
    cosine = jnp.cos(angles)
    sine = jnp.sin(angles)
    sine = jnp.where(lane < half, -sine, sine)
    proj = []
    for t in range(3):
        acc = None
        for k in range(pieces):
            loads["qkv", t, k].wait()
            term = product(normed[:, k * span:(k + 1) * span], qkv[t, k * span:(k + 1) * span, :])
            acc = term if acc is None else acc + term
        if t == 1:
            load("emb", emb_hbm, emb)
            load("din", din_hbm, din)
            load("dqkv", dqkv_hbm, dqkv)
            load("dout", dout_hbm, dout)
            load("headw", headw_hbm, headw)
        if t < 2:
            turned = []
            for h in range(heads):
                one = acc[:, h * HEAD_DIM:(h + 1) * HEAD_DIM]
                turned.append(one * cosine + pltpu.roll(one, half, 1) * sine)
            acc = jnp.concatenate(turned, axis=1)
        proj.append(acc.astype(bf).astype(jnp.float32))

    factor = 1.0 / math.sqrt(HEAD_DIM)
    loads["keys"].wait()
    loads["values"].wait()
    group = 8
    padded = 8
    owner = lax.broadcasted_iota(jnp.int32, (group, padded, cols), 2) // HEAD_DIM
    mine = owner == lax.broadcasted_iota(jnp.int32, (group, padded, cols), 1)
    place = lax.broadcasted_iota(jnp.int32, (group, padded, cache_len), 2).astype(jnp.float32)
    mixed = []
    for g in range(s_local // group):
        at = slice(g * group, (g + 1) * group)
        q_g = jnp.where(mine, proj[0][at][:, None, :], 0.0)
        scores = lax.dot_general(
            q_g.astype(bf), keys[at], (((2,), (2,)), ((0,), (0,))),
            preferred_element_type=jnp.float32,
        ) * factor
        own_score = jnp.sum(q_g * proj[1][at][:, None, :], axis=-1, keepdims=True) * factor
        live = place < lens[at, :cache_len][:, None, :]
        scores = jnp.where(live, scores, -jnp.inf)
        highest = jnp.maximum(jnp.max(scores, axis=-1, keepdims=True), own_score)
        expo = jnp.exp(scores - highest)
        own_expo = jnp.exp(own_score - highest)
        totals = jnp.sum(expo, axis=-1, keepdims=True) + own_expo
        weights = (expo / totals).astype(bf)
        own_weight = (own_expo / totals).astype(bf).astype(jnp.float32)
        out = lax.dot_general(
            weights, values[at], (((2,), (1,)), ((0,), (0,))),
            preferred_element_type=jnp.float32,
        )
        out = jnp.where(mine, out + own_weight * proj[2][at][:, None, :], 0.0)
        mixed.append(jnp.sum(out, axis=1))
    mixed = jnp.concatenate(mixed, axis=0).astype(bf)

    loads["outw"].wait()
    slim = width // n
    pl.semaphore_wait(barrier, n)

    def row_block(j):
        return product(mixed, outw[:, pl.ds(pl.multiple_of(j * slim, slim), slim)])

    summed = summed_over_tp(0, row_block, tbuf)

    vocab = emb.shape[1]
    loads["emb"].wait()
    ids = lax.broadcasted_iota(jnp.int32, (vocab, streams), 0) + me * vocab
    for c in range(codes):
        onehot = jnp.where(tokens_ref[c:c + 1, :] == ids, 1.0, 0.0).astype(bf)
        looked_up = lax.dot_general(
            onehot, emb[c], (((0,), (0,)), ((), ())), preferred_element_type=jnp.float32
        )
        for a in range(2):
            ent[lax.rem(a + sec, 2), c * s_local:(c + 1) * s_local, :] = looked_up[
                a * s_local:(a + 1) * s_local
            ]
    loads["din"].wait()

    summed = finished(0, summed, tbuf)
    start = pl.multiple_of(me * slim, slim)
    temporal = (hidden_ref[:, pl.ds(start, slim)].astype(jnp.float32) + summed).astype(bf)
    temporal_ref[...] = temporal
    rows[0] = temporal
    row_swap = to_partner(0, rows.at[0], rows.at[1])
    row_swap.start()

    part = din.shape[2] // n
    share = headw.shape[2] // n
    lanes = dqkv.shape[3]

    def at_code(c):
        return slice(c * s_local, (c + 1) * s_local)

    def features(j):
        return pl.ds(pl.multiple_of(j * part, part), part)

    class Reduction:
        def __init__(self, phase, a, block_of, buf):
            self.phase, self.a, self.block_of, self.buf = phase, a, block_of, buf
            self.firsts = {}

        def send(self, stage, i, h, at, peer):
            spot_of = (self.a, i, at)
            copy = to_peer(
                2 * self.phase + stage, self.a if stage else 4 * i + 2 * h + self.a,
                self.buf.at[(2 * stage, *spot_of)], self.buf.at[(2 * stage + 1, *spot_of)], peer,
            )
            copy.start()
            return copy

        def start(self):
            for i, d in enumerate(order + [0]):
                target = lax.rem(spot + d, half_n)
                self.buf[0, self.a, i] = self.block_of(2 * target + 1 - pair).astype(bf)
                for h, at in halves(self.buf.shape[3]):
                    self.firsts[i, h] = self.send(0, i, h, at, mate)

        def forward(self):
            for i, d in enumerate(order + [0]):
                target = lax.rem(spot + d, half_n)
                block = self.block_of(2 * target + pair)
                added = []
                for h, at in halves(self.buf.shape[3]):
                    self.firsts[i, h].wait_recv()
                    added.append(block[at] + self.buf[1, self.a, i, at].astype(jnp.float32))
                    if d:
                        self.buf[2, self.a, i, at] = added[-1].astype(bf)
                        self.send(1, i, h, at, 2 * target + pair)
            self.own = jnp.concatenate(added, axis=0)

        def result(self):
            block = self.own
            all_came(2 * self.phase + 1, self.a, self.buf.at[3, self.a, pl.ds(0, half_n - 1)])
            for i in range(half_n - 1):
                block = block + self.buf[3, self.a, i].astype(jnp.float32)
            return block

        def drain(self):
            all_sent(2 * self.phase, self.buf.at[0, self.a])
            all_sent(2 * self.phase + 1, self.buf.at[2, self.a, pl.ds(0, half_n - 1)])

    def entry_block(a):
        def block_of(j):
            terms = [product(rows[a], din[c, :, features(j)]) for c in range(codes)]
            return ent[a, :, features(j)] + jnp.concatenate(terms, axis=0)
        return block_of

    def row_squares(block):
        return lax.dot_general(
            jnp.ones((8, part), jnp.float32), block * block, (((1,), (1,)), ((), ())),
            preferred_element_type=jnp.float32, precision=lax.Precision.HIGHEST,
        )

    def squares_out(which, a, block):
        squares[which, a, me] = row_squares(block)
        for d in range(1, n):
            to_peer(
                8 + which + 4 * a, 0, squares.at[which, a, me], squares.at[which, a, me],
                lax.rem(me + d, n),
            ).start()

    def row_factor(which, a):
        all_came(8 + which + 4 * a, 0, squares.at[which, a, pl.ds(0, n - 1)])
        mean = jnp.sum(squares[which, a], axis=0) / (n * part)
        column = lax.dot_general(
            mean, jnp.full((8, 128), 0.125, jnp.float32), (((0,), (0,)), ((), ())),
            preferred_element_type=jnp.float32, precision=lax.Precision.HIGHEST,
        )
        return lax.rsqrt(column + EPSILON)

    class Gather:
        def __init__(self, a):
            self.a = a
            self.copies = []

        def send(self, phase, i, place, peer):
            there = nrm.at[place, self.a]
            copy = to_peer(phase, 2 * i + self.a, there, there, peer)
            copy.start()
            return copy

        def start(self, block):
            nrm[me, self.a] = (block * dgain_ref[:, features(me)]).astype(bf)
            for i, d in enumerate(order):
                peer = 2 * lax.rem(spot + d, half_n) + pair
                self.copies.append(self.send(6, i, me, peer))
            self.send(7, 0, me, mate)

        def forward(self):
            for i, d in enumerate(order):
                came = 2 * lax.rem(spot - d + half_n, half_n) + pair
                self.copies[i].wait_recv()
                self.send(7, 0, came, mate)

    def projections(a, r):
        all_came(7, a, nrm.at[pl.ds(0, half_n), a])
        chunk = lax.rem(a + sec, 2)
        for c in range(codes):
            x = jnp.concatenate([nrm[j, a, at_code(c), :] for j in range(n)], axis=1)
            f = r[at_code(c)]
            qs[chunk, c] = (product(x, dqkv[c, 0]) * f).astype(bf)
            kvs[chunk, 0, c] = (product(x, dqkv[c, 1]) * f).astype(bf)
            kvs[chunk, 1, c] = (product(x, dqkv[c, 2]) * f).astype(bf)
        to_partner(1 + chunk, kvs.at[chunk], kvr.at[chunk]).start()

    row_head = lax.rem(lax.broadcasted_iota(jnp.int32, (2 * lanes, lanes), 0), lanes) // DEPTH_HDIM
    col_head = lax.broadcasted_iota(jnp.int32, (2 * lanes, lanes), 1) // DEPTH_HDIM
    ones = jnp.where(row_head == col_head, 1.0, 0.0).astype(bf)
    scale = 1.0 / math.sqrt(DEPTH_HDIM)

    def scores(queries, keys):
        both = jnp.concatenate(
            [query * key.astype(jnp.float32) for query, key in zip(queries, keys)], axis=0
        )
        high = both.astype(bf)
        low = (both - high.astype(jnp.float32)).astype(bf)
        out = product(jnp.concatenate([high, low], axis=1), ones) * scale
        return [out[i * s_local:(i + 1) * s_local] for i in range(len(queries))]

    partner_swaps = [row_swap]

    def attention(a):
        queries = [qs[a, c].astype(jnp.float32) for c in range(codes)]
        pairs = [(q, k) for q in range(codes) for k in range(q + 1)]
        local = scores([queries[q] for q, _ in pairs], [kvs[a, 0, k] for _, k in pairs])
        local = dict(zip(pairs, local))
        swap = to_partner(1 + a, kvs.at[a], kvr.at[a])
        swap.wait_recv()
        partner_swaps.append(swap)
        pairs = [(q, k) for q in range(codes) for k in range(codes)]
        prior = scores([queries[q] for q, _ in pairs], [kvr[a, 0, k] for _, k in pairs])
        prior = dict(zip(pairs, prior))
        for q in range(codes):
            every = [jnp.where(sec > 0, prior[q, k], -jnp.inf) for k in range(codes)]
            every += [local[q, k] for k in range(q + 1)]
            top = every[0]
            for item in every[1:]:
                top = jnp.maximum(top, item)
            expo = [jnp.exp(item - top) for item in every]
            sums = expo[0]
            for item in expo[1:]:
                sums = sums + item
            out = None
            for k, item in enumerate(expo):
                value = kvr[a, 1, k] if k < codes else kvs[a, 1, k - codes]
                term = (item / sums).astype(bf).astype(jnp.float32) * value.astype(jnp.float32)
                out = term if out is None else out + term
            mix[a, at_code(q), :] = out.astype(bf)

    def resid_block(a):
        def block_of(j):
            return jnp.concatenate(
                [product(mix[a, at_code(c), :], dout[c, :, features(j)]) for c in range(codes)],
                axis=0,
            )
        return block_of

    def vocab_block(hidden):
        def block_of(j):
            there = pl.ds(pl.multiple_of(j * share, share), share)
            return jnp.concatenate(
                [product(hidden[at_code(c), :], headw[c, :, there]) for c in range(codes)],
                axis=0,
            )
        return block_of

    entries = [Reduction(1, a, entry_block(a), ebuf) for a in range(2)]
    entries[0].start()
    row_swap.wait_recv()
    entries[1].start()
    entries[0].forward()
    entries[1].forward()
    gathers = [Gather(a) for a in range(2)]
    for a in range(2):
        block = entries[a].result()
        squares_out(0, a, block)
        gathers[a].start(block)
        entry[lax.rem(a + sec, 2)] = block
    gathers[0].forward()
    gathers[1].forward()
    loads["dqkv"].wait()
    loads["dout"].wait()
    for a in range(2):
        factor = row_factor(0, a)
        projections(a, factor)
    resids = [Reduction(2, a, resid_block(a), dbuf) for a in range(2)]
    for a in range(2):
        attention(a)
        resids[a].start()
    resids[0].forward()
    resids[1].forward()
    loads["headw"].wait()
    heads_of = []
    for a in range(2):
        resid = entry[a] + resids[a].result()
        squares_out(1, a, resid)
        hidden = (resid * hgain_ref[:, features(me)]).astype(bf)
        heads_of.append(Reduction(5, a, vocab_block(hidden), lbuf))
        heads_of[a].start()
    heads_of[0].forward()
    factors = [row_factor(1, a) for a in range(2)]
    heads_of[1].forward()
    for a in range(2):
        out = heads_of[a].result() * factors[a][:, :1]
        logits_ref[:, a * s_local:(a + 1) * s_local, :] = out.reshape(codes, s_local, share)
    all_sent(0, tbuf.at[0])
    all_sent(1, tbuf.at[2, pl.ds(0, half_n - 1)])
    for item in entries + resids + heads_of:
        item.drain()
    all_sent(6, nrm.at[pl.ds(0, half_n - 1)])
    all_sent(7, nrm.at[pl.ds(0, half_n)])
    for which in range(2):
        for a in range(2):
            all_sent(8 + which + 4 * a, squares.at[which, a, pl.ds(0, n - 1)])
    for copy in partner_swaps:
        copy.wait_send()
    assert len(arrivals) <= recv_sem.shape[0]


def deliver_kernel(temporal_ref, logits_ref, temporal_hbm, logits_hbm, turned, sems):
    first = pltpu.make_async_copy(temporal_ref, temporal_hbm, sems.at[0])
    first.start()
    turned[...] = jnp.swapaxes(logits_ref[...], 0, 1)
    second = pltpu.make_async_copy(turned, logits_hbm, sems.at[1])
    second.start()
    first.wait()
    second.wait()


def fused(
    n, hidden_in, temporal_gain, temporal_qkv, temporal_out_weight, cache_keys, cache_values,
    lengths, depth_in, depth_embed, depth_gain, depth_qkv, depth_out_weight, head_gain,
    head_weight, tokens,
):
    s_local, width = hidden_in.shape
    codes, slim, deep = depth_in.shape
    streams = 2 * s_local
    total = codes * streams
    lanes = depth_qkv.shape[3]
    part = head_weight.shape[1]
    share = head_weight.shape[2] // n
    bf, f32 = jnp.bfloat16, jnp.float32
    pieces = 4
    big = [temporal_qkv, cache_keys, cache_values, temporal_out_weight, depth_in, depth_embed,
           depth_qkv, depth_out_weight, head_weight]
    vmem = pl.BlockSpec(memory_space=pltpu.VMEM)
    scratch = [pltpu.VMEM(a.shape, a.dtype) for a in big] + [
        pltpu.VMEM((4, n // 2, s_local, slim), bf),
        pltpu.VMEM((2, s_local, slim), bf),
        pltpu.VMEM((2, total // 2, deep), f32),
        pltpu.VMEM((4, 2, n // 2, total // 2, part), bf),
        pltpu.VMEM((n, 2, total // 2, part), bf),
        pltpu.VMEM((2, 2, codes, s_local, lanes), bf),
        pltpu.VMEM((2, 2, codes, s_local, lanes), bf),
        pltpu.VMEM((2, total // 2, lanes), bf),
        pltpu.VMEM((4, 2, n // 2, total // 2, part), bf),
        pltpu.VMEM((4, 2, n // 2, total // 2, share), bf),
        pltpu.VMEM((2, 2, n, 8, total // 2), f32),
        pltpu.VMEM((2, codes, s_local, lanes), bf),
        pltpu.VMEM((2, total // 2, part), f32),
        pltpu.SemaphoreType.DMA((3 * pieces + 8,)),
        pltpu.SemaphoreType.DMA((14,)),
        pltpu.SemaphoreType.DMA((7 * n + 4,)),
        pltpu.SemaphoreType.DMA((3,)),
        pltpu.SemaphoreType.DMA((3,)),
    ]
    temporal, logits = pl.pallas_call(
        functools.partial(tick_kernel, n, pieces),
        out_shape=(
            pltpu.VMEM((s_local, slim), bf),
            pltpu.VMEM((codes, streams, share), f32),
        ),
        in_specs=[vmem] * 6 + [pl.BlockSpec(memory_space=pl.ANY)] * 9,
        out_specs=(vmem, vmem),
        scratch_shapes=scratch,
        compiler_params=pltpu.CompilerParams(
            collective_id=0, has_side_effects=True, vmem_limit_bytes=60 * 1024 * 1024
        ),
    )(
        hidden_in, temporal_gain[None, :], lengths[None, :], tokens.T, depth_gain[None, :], head_gain[None, :],
        *big,
    )
    return pl.pallas_call(
        deliver_kernel,
        out_shape=(
            jax.ShapeDtypeStruct((s_local, slim), bf),
            jax.ShapeDtypeStruct((streams, codes, share), f32),
        ),
        in_specs=[vmem] * 2,
        out_specs=(pl.BlockSpec(memory_space=pl.ANY),) * 2,
        scratch_shapes=[
            pltpu.VMEM((streams, codes, share), f32),
            pltpu.SemaphoreType.DMA((2,)),
        ],
        compiler_params=pltpu.CompilerParams(vmem_limit_bytes=2 * 1024 * 1024),
    )(temporal, logits)


def fits(n, arrays):
    hidden_in, depth_in, depth_qkv = arrays[0], arrays[7], arrays[10]
    total = depth_in.shape[0] * 2 * hidden_in.shape[0]
    return (
        lax.axis_size("section") == 2
        and depth_qkv.shape[3] == 128
        and arrays[13].shape[1] % 128 == 0
        and arrays[13].shape[2] % (128 * n) == 0
        and n % 2 == 0
        and total % 256 == 0
        and hidden_in.shape[0] % 16 == 0
        and arrays[4].shape[1] <= HEAD_DIM
        and arrays[2].shape[2] <= 8 * HEAD_DIM
    )


def any_size(*arrays):
    n = lax.axis_size("tp")
    if fits(n, arrays):
        return fused(n, *arrays)
    return per_device(*arrays)


def solution(mesh):
    return jax.shard_map(
        any_size,
        mesh=mesh,
        in_specs=(
            P(("grp", "section"), None),
            P(),
            P(None, None, "tp"),
            P("tp", None),
            P(("grp", "section"), None, "tp"),
            P(("grp", "section"), None, "tp"),
            P(("grp", "section")),
            P("section", "tp", None),
            P("section", "tp", None),
            P(),
            P("section", None, None, "tp"),
            P("section", "tp", None),
            P(),
            P("section", "tp", None),
            P("grp", "section"),
        ),
        out_specs=(P(("grp", "section"), "tp"), P("grp", "section", "tp")),
        check_vma=False,
    )
```

```python
import functools
import math

import jax
import jax.numpy as jnp
from jax import lax
from jax.experimental import pallas as pl
from jax.experimental.pallas import tpu as pltpu
from jax.sharding import PartitionSpec as P

HEAD_DIM = 128
DEPTH_HDIM = 64


EPSILON = 1e-05


def passed_along(block, axis, distance):
    devices = range(lax.axis_size(axis))
    route = [(i - distance, i) for i in devices if i - distance in devices]
    return lax.ppermute(block, axis, route)


def from_partner(shard, axis, distance):
    return lax.ppermute(shard, axis, [(i, i ^ 1 << distance) for i in range(lax.axis_size(axis))])


def rms_norm(values, scale):
    wide = values.astype(jnp.float32)
    return wide * lax.rsqrt(jnp.mean(wide * wide, axis=-1, keepdims=True) + EPSILON) * scale


def rotate(vectors, positions):
    halfdim = vectors.shape[-1] // 2
    spacing = jnp.arange(halfdim, dtype=jnp.float32) / halfdim
    inverse = jnp.exp(-math.log(10000.0) * spacing)
    angles = positions.astype(jnp.float32)[:, None, None] * inverse[None, None, :]
    cosine = jnp.cos(angles)
    sine = jnp.sin(angles)
    first = vectors[..., :halfdim]
    second = vectors[..., halfdim:]
    return jnp.concatenate(
        [first * cosine - second * sine, first * sine + second * cosine], axis=-1
    )


def per_device(
    hidden_in,
    temporal_gain,
    temporal_qkv,
    temporal_out_weight,
    cache_keys,
    cache_values,
    lengths,
    depth_in,
    depth_embed,
    depth_gain,
    depth_qkv,
    depth_out_weight,
    head_gain,
    head_weight,
    tokens,
):
    local_streams = hidden_in.shape[0]
    local_cols = temporal_qkv.shape[2]
    local_heads = local_cols // HEAD_DIM
    cache_len = cache_keys.shape[1]
    normed = rms_norm(hidden_in, temporal_gain).astype(jnp.bfloat16)
    projected = jnp.einsum("sd,tdf->tsf", normed, temporal_qkv, preferred_element_type=jnp.float32)
    layout = (local_streams, local_heads, HEAD_DIM)
    queries = rotate(projected[0].reshape(layout), lengths).astype(jnp.bfloat16)
    keys_new = rotate(projected[1].reshape(layout), lengths).astype(jnp.bfloat16)
    values_new = projected[2].reshape(layout).astype(jnp.bfloat16)
    cached_keys = cache_keys.reshape(local_streams, cache_len, local_heads, HEAD_DIM)
    cached_values = cache_values.reshape(local_streams, cache_len, local_heads, HEAD_DIM)
    factor = 1.0 / math.sqrt(HEAD_DIM)
    scores = (
        jnp.einsum("shd,sphd->shp", queries, cached_keys, preferred_element_type=jnp.float32)
        * factor
    )
    own_score = (
        jnp.sum(queries.astype(jnp.float32) * keys_new.astype(jnp.float32), axis=-1) * factor
    )
    valid = jnp.arange(cache_len, dtype=jnp.int32)[None, None, :] < lengths[:, None, None]
    scores = jnp.where(valid, scores, -jnp.inf)
    highest = jnp.maximum(jnp.max(scores, axis=-1), own_score)
    expo = jnp.exp(scores - highest[..., None])
    own_expo = jnp.exp(own_score - highest)
    totals = jnp.sum(expo, axis=-1) + own_expo
    weights = (expo / totals[..., None]).astype(jnp.bfloat16)
    own_weight = (own_expo / totals).astype(jnp.bfloat16)
    mixed = jnp.einsum("shp,sphd->shd", weights, cached_values, preferred_element_type=jnp.float32)
    mixed = mixed + own_weight.astype(jnp.float32)[..., None] * values_new.astype(jnp.float32)
    mixed = mixed.astype(jnp.bfloat16).reshape(local_streams, local_cols)
    partial_rows = jnp.dot(mixed, temporal_out_weight, preferred_element_type=jnp.float32)
    summed = lax.psum_scatter(partial_rows, "tp", scatter_dimension=1, tiled=True)
    slice_width = summed.shape[1]
    tp_place = lax.axis_index("tp")
    resid_in = lax.dynamic_slice_in_dim(hidden_in, tp_place * slice_width, slice_width, 1)
    temporal = (resid_in.astype(jnp.float32) + summed).astype(jnp.bfloat16)
    all_rows = lax.all_gather(temporal, "section", axis=0, tiled=True)
    streams = all_rows.shape[0]
    codes = depth_in.shape[0]
    entry_part = jnp.einsum("sd,cde->sce", all_rows, depth_in, preferred_element_type=jnp.float32)
    vocab_local = depth_embed.shape[1]
    first_id = tp_place * vocab_local
    onehot = (
        tokens[:, :, None] == first_id + jnp.arange(vocab_local, dtype=jnp.int32)[None, None, :]
    ).astype(jnp.bfloat16)
    embedded = jnp.einsum("scv,cve->sce", onehot, depth_embed, preferred_element_type=jnp.float32)
    entry_terms = entry_part + embedded
    hidden_rows = head_weight.shape[1]
    hidden_start = tp_place * hidden_rows
    entry = lax.psum(entry_terms, "tp")
    depth_normed = rms_norm(entry, depth_gain).astype(jnp.bfloat16)
    dproj = jnp.einsum(
        "sce,ctef->tscf", depth_normed, depth_qkv, preferred_element_type=jnp.float32
    ).astype(jnp.bfloat16)
    prior_keys, prior_values = passed_along((dproj[1], dproj[2]), "section", 1)
    depth_cols = dproj.shape[3]
    head_part = min(depth_cols, DEPTH_HDIM)
    local_parts = depth_cols // head_part
    sharers = DEPTH_HDIM // head_part
    all_keys = jnp.concatenate([prior_keys, dproj[1]], axis=1).reshape(
        streams, 2 * codes, local_parts, head_part
    )
    all_values = jnp.concatenate([prior_values, dproj[2]], axis=1).reshape(
        streams, 2 * codes, local_parts, head_part
    )
    depth_queries = dproj[0].reshape(streams, codes, local_parts, head_part)
    depth_scores = jnp.einsum(
        "sqhd,skhd->shqk", depth_queries, all_keys, preferred_element_type=jnp.float32
    )
    for level in range(sharers.bit_length() - 1):
        depth_scores = depth_scores + from_partner(depth_scores, "tp", level)
    depth_scores = depth_scores * (1.0 / math.sqrt(DEPTH_HDIM))
    section_place = lax.axis_index("section")
    query_pos = jnp.arange(codes, dtype=jnp.int32)[:, None]
    key_pos = jnp.arange(2 * codes, dtype=jnp.int32)[None, :]
    allowed = jnp.where(key_pos < codes, section_place > 0, key_pos - codes <= query_pos)
    depth_scores = jnp.where(allowed[None, None], depth_scores, -jnp.inf)
    depth_top = jnp.max(depth_scores, axis=-1, keepdims=True)
    depth_expo = jnp.exp(depth_scores - depth_top)
    depth_weights = (depth_expo / jnp.sum(depth_expo, axis=-1, keepdims=True)).astype(jnp.bfloat16)
    depth_mixed = jnp.einsum(
        "shqk,skhd->sqhd", depth_weights, all_values, preferred_element_type=jnp.float32
    ).astype(jnp.bfloat16)
    depth_mixed = depth_mixed.reshape(streams, codes, depth_cols)
    depth_terms = jnp.einsum(
        "scf,cfe->sce", depth_mixed, depth_out_weight, preferred_element_type=jnp.float32
    )
    resid = entry + lax.psum(depth_terms, "tp")
    head_normed = rms_norm(resid, head_gain).astype(jnp.bfloat16)
    own_hidden = lax.dynamic_slice_in_dim(head_normed, hidden_start, hidden_rows, 2)
    partial_logits = jnp.einsum(
        "sce,cev->scv", own_hidden, head_weight, preferred_element_type=jnp.float32
    )
    logits = lax.psum_scatter(partial_logits, "tp", scatter_dimension=2, tiled=True)
    return (temporal, logits)


MESH = pl.DeviceIdType.MESH


def normalised(wide, scale):
    return wide * lax.rsqrt(jnp.mean(wide * wide, axis=-1, keepdims=True) + EPSILON) * scale


def product(left, right):
    return jnp.dot(left, right, preferred_element_type=jnp.float32)


def tick_kernel(
    n, pieces,
    hidden_hbm, gain_hbm, lens_hbm, tokens_hbm, dgain_hbm, hgain_hbm,
    qkv_hbm, keys_hbm, values_hbm, outw_hbm, din_hbm, emb_hbm, dqkv_hbm, dout_hbm, headw_hbm,
    temporal_ref, logits_ref,
    hidden_ref, gain_ref, lens_ref, tokens_ref, dgain_ref, hgain_ref,
    qkv, keys, values, outw, din, emb, dqkv, dout, headw,
    tbuf, rows, ent, ebuf, nrm, kvs, kvr, mix, dbuf, lbuf, squares, qs, entry,
    load_sem, send_sem, recv_sem, pair_send, pair_recv,
):
    me = lax.axis_index("tp")
    sec = lax.axis_index("section")
    s_local, width = hidden_ref.shape
    cols = qkv.shape[2]
    heads = cols // HEAD_DIM
    cache_len = keys.shape[1]
    codes = din.shape[0]
    streams = 2 * s_local
    bf = jnp.bfloat16

    span = width // pieces
    loads = {}
    slot = 0

    def load(name, source, target):
        nonlocal slot
        loads[name] = pltpu.make_async_copy(source, target, load_sem.at[slot])
        loads[name].start()
        slot += 1

    def load_weights(t):
        for k in range(pieces):
            part = pl.ds(k * span, span)
            load(("qkv", t, k), qkv_hbm.at[t, part, :], qkv.at[t, part, :])

    load("hidden", hidden_hbm, hidden_ref)
    load("gain", gain_hbm, gain_ref)
    load("lens", lens_hbm, lens_ref)
    load_weights(0)
    load("keys", keys_hbm, keys)
    load_weights(1)
    load("values", values_hbm, values)
    load_weights(2)
    load("outw", outw_hbm, outw)
    load("tokens", tokens_hbm, tokens_ref)
    load("dgain", dgain_hbm, dgain_ref)
    load("hgain", hgain_hbm, hgain_ref)
    barrier = pltpu.get_barrier_semaphore()
    for d in range(1, n):
        pl.semaphore_signal(
            barrier, inc=1, device_id={"tp": lax.rem(me + d, n)}, device_id_type=MESH
        )
    pl.semaphore_signal(barrier, inc=1, device_id={"section": 1 - sec}, device_id_type=MESH)

    arrivals = {}

    def arrival(phase, d):
        if phase == 10:
            phase = 2
        return arrivals.setdefault((phase, d), len(arrivals))

    def to_peer(phase, d, source, target, peer):
        return pltpu.make_async_remote_copy(
            src_ref=source, dst_ref=target,
            send_sem=send_sem.at[phase], recv_sem=recv_sem.at[arrival(phase, d)],
            device_id={"tp": peer}, device_id_type=MESH,
        )

    def all_came(phase, d, there):
        to_peer(phase, d, there, there, mate).wait_recv()

    def all_sent(phase, sent):
        to_peer(phase, 0, sent, sent, mate).wait_send()

    def to_partner(phase, source, target):
        return pltpu.make_async_remote_copy(
            src_ref=source, dst_ref=target,
            send_sem=pair_send.at[phase], recv_sem=pair_recv.at[phase],
            device_id={"section": 1 - sec}, device_id_type=MESH,
        )

    half_n = n // 2
    pair = lax.rem(me, 2)
    spot = me // 2
    mate = 2 * spot + 1 - pair
    order = sorted(range(1, half_n), key=lambda d: abs(d - half_n // 2))

    def halves(size):
        return [(h, slice(h * size // 2, (h + 1) * size // 2)) for h in range(2)]

    def summed_over_tp(phase, block_of, buf):
        firsts = []
        parts = halves(buf.shape[2])
        for i, d in enumerate(order + [0]):
            target = lax.rem(spot + d, half_n)
            buf[0, i] = block_of(2 * target + 1 - pair).astype(bf)
            for h, at in parts:
                firsts.append(
                    to_peer(2 * phase, 2 * i + h, buf.at[0, i, at], buf.at[1, i, at], mate)
                )
                firsts[-1].start()
        for i, d in enumerate(order + [0]):
            target = lax.rem(spot + d, half_n)
            block = block_of(2 * target + pair)
            added = []
            for h, at in parts:
                firsts[2 * i + h].wait_recv()
                added.append(block[at] + buf[1, i, at].astype(jnp.float32))
                if d:
                    buf[2, i, at] = added[-1].astype(bf)
                    to_peer(
                        2 * phase + 1, 0, buf.at[2, i, at], buf.at[3, i, at], 2 * target + pair
                    ).start()
        return jnp.concatenate(added, axis=0)

    def finished(phase, block, buf):
        all_came(2 * phase + 1, 0, buf.at[3, pl.ds(0, half_n - 1)])
        for i in range(half_n - 1):
            block = block + buf[3, i].astype(jnp.float32)
        return block

    for name in ("hidden", "gain", "lens"):
        loads[name].wait()
    normed = normalised(hidden_ref[...].astype(jnp.float32), gain_ref[...]).astype(bf)
    half = HEAD_DIM // 2
    lane = lax.broadcasted_iota(jnp.int32, (s_local, HEAD_DIM), 1)
    spacing = lax.rem(lane, half).astype(jnp.float32) / half
    diagonal = lax.broadcasted_iota(jnp.int32, (s_local, s_local), 0) == lax.broadcasted_iota(
        jnp.int32, (s_local, s_local), 1
    )
    lens = jnp.sum(
        jnp.where(diagonal, lens_ref[...].astype(jnp.float32), 0.0), axis=1, keepdims=True
    )
    lens = jnp.broadcast_to(lens, (s_local, HEAD_DIM))
    angles = lens * jnp.exp(-math.log(10000.0) * spacing)
    cosine = jnp.cos(angles)
    sine = jnp.sin(angles)
    sine = jnp.where(lane < half, -sine, sine)

    def projected(t):
        acc = None
        for k in range(pieces):
            loads["qkv", t, k].wait()
            term = product(normed[:, k * span:(k + 1) * span], qkv[t, k * span:(k + 1) * span, :])
            acc = term if acc is None else acc + term
        if t < 2:
            turned = []
            for h in range(heads):
                one = acc[:, h * HEAD_DIM:(h + 1) * HEAD_DIM]
                turned.append(one * cosine + pltpu.roll(one, half, 1) * sine)
            acc = jnp.concatenate(turned, axis=1)
        return acc.astype(bf).astype(jnp.float32)

    factor = 1.0 / math.sqrt(HEAD_DIM)
    group = 8
    padded = 8
    owner = lax.broadcasted_iota(jnp.int32, (group, padded, cols), 2) // HEAD_DIM
    mine = owner == lax.broadcasted_iota(jnp.int32, (group, padded, cols), 1)
    place = lax.broadcasted_iota(jnp.int32, (group, padded, cache_len), 2).astype(jnp.float32)
    groups = [slice(g * group, (g + 1) * group) for g in range(s_local // group)]

    queries = projected(0)
    loads["keys"].wait()
    cached = []
    for at in groups:
        q_g = jnp.where(mine, queries[at][:, None, :], 0.0)
        cached.append(
            lax.dot_general(
                q_g.astype(bf), keys[at], (((2,), (2,)), ((0,), (0,))),
                preferred_element_type=jnp.float32,
            ) * factor
        )
    new_keys = projected(1)
    load("emb", emb_hbm, emb)
    load("din", din_hbm, din)
    load("dqkv", dqkv_hbm, dqkv)
    load("dout", dout_hbm, dout)
    load("headw", headw_hbm, headw)
    weights, own_weights = [], []
    for at, scores in zip(groups, cached):
        own_score = jnp.sum(
            jnp.where(mine, (queries[at] * new_keys[at])[:, None, :], 0.0), axis=-1, keepdims=True
        ) * factor
        live = place < lens[at, :cache_len][:, None, :]
        scores = jnp.where(live, scores, -jnp.inf)
        highest = jnp.maximum(jnp.max(scores, axis=-1, keepdims=True), own_score)
        expo = jnp.exp(scores - highest)
        own_expo = jnp.exp(own_score - highest)
        totals = jnp.sum(expo, axis=-1, keepdims=True) + own_expo
        weights.append((expo / totals).astype(bf))
        own_weight = (own_expo / totals).astype(bf).astype(jnp.float32)
        own_weights.append(jnp.sum(jnp.where(mine, own_weight, 0.0), axis=1))
    loads["values"].wait()
    mixed = []
    for at, weight in zip(groups, weights):
        out = lax.dot_general(
            weight, values[at], (((2,), (1,)), ((0,), (0,))), preferred_element_type=jnp.float32
        )
        mixed.append(jnp.sum(jnp.where(mine, out, 0.0), axis=1))
    mixed = jnp.concatenate(mixed, axis=0)
    own_weights = jnp.concatenate(own_weights, axis=0)
    mixed = (mixed + own_weights * projected(2)).astype(bf)

    loads["outw"].wait()
    slim = width // n
    pl.semaphore_wait(barrier, n)

    def row_block(j):
        return product(mixed, outw[:, pl.ds(pl.multiple_of(j * slim, slim), slim)])

    summed = summed_over_tp(0, row_block, tbuf)

    vocab = emb.shape[1]
    for name in ("emb", "tokens", "dgain", "hgain"):
        loads[name].wait()
    ids = lax.broadcasted_iota(jnp.int32, (vocab, streams), 0) + me * vocab
    for c in range(codes):
        onehot = jnp.where(tokens_ref[c:c + 1, :] == ids, 1.0, 0.0).astype(bf)
        looked_up = lax.dot_general(
            onehot, emb[c], (((0,), (0,)), ((), ())), preferred_element_type=jnp.float32
        )
        for a in range(2):
            ent[lax.rem(a + sec, 2), c * s_local:(c + 1) * s_local, :] = looked_up[
                a * s_local:(a + 1) * s_local
            ]
    loads["din"].wait()

    summed = finished(0, summed, tbuf)
    start = pl.multiple_of(me * slim, slim)
    temporal = (hidden_ref[:, pl.ds(start, slim)].astype(jnp.float32) + summed).astype(bf)
    temporal_ref[...] = temporal
    rows[0] = temporal
    row_swap = to_partner(0, rows.at[0], rows.at[1])
    row_swap.start()

    part = din.shape[2] // n
    share = headw.shape[2] // n
    lanes = dqkv.shape[3]

    def at_code(c):
        return slice(c * s_local, (c + 1) * s_local)

    def features(j):
        return pl.ds(pl.multiple_of(j * part, part), part)

    class Reduction:
        def __init__(self, phase, a, block_of, buf):
            self.phase, self.a, self.block_of, self.buf = phase, a, block_of, buf
            self.firsts = {}

        def send(self, stage, i, h, at, peer):
            spot_of = (self.a, i, at)
            copy = to_peer(
                2 * self.phase + stage, self.a if stage else 4 * i + 2 * h + self.a,
                self.buf.at[(2 * stage, *spot_of)], self.buf.at[(2 * stage + 1, *spot_of)], peer,
            )
            copy.start()
            return copy

        def start(self):
            for i, d in enumerate(order + [0]):
                target = lax.rem(spot + d, half_n)
                self.buf[0, self.a, i] = self.block_of(2 * target + 1 - pair).astype(bf)
                for h, at in halves(self.buf.shape[3]):
                    self.firsts[i, h] = self.send(0, i, h, at, mate)

        def forward(self):
            for i, d in enumerate(order + [0]):
                target = lax.rem(spot + d, half_n)
                block = self.block_of(2 * target + pair)
                added = []
                for h, at in halves(self.buf.shape[3]):
                    self.firsts[i, h].wait_recv()
                    added.append(block[at] + self.buf[1, self.a, i, at].astype(jnp.float32))
                    if d:
                        self.buf[2, self.a, i, at] = added[-1].astype(bf)
                        self.send(1, i, h, at, 2 * target + pair)
            self.own = jnp.concatenate(added, axis=0)

        def result(self):
            block = self.own
            all_came(2 * self.phase + 1, self.a, self.buf.at[3, self.a, pl.ds(0, half_n - 1)])
            for i in range(half_n - 1):
                block = block + self.buf[3, self.a, i].astype(jnp.float32)
            return block

        def drain(self):
            all_sent(2 * self.phase, self.buf.at[0, self.a])
            all_sent(2 * self.phase + 1, self.buf.at[2, self.a, pl.ds(0, half_n - 1)])

    def entry_block(a):
        def block_of(j):
            terms = [product(rows[a], din[c, :, features(j)]) for c in range(codes)]
            return ent[a, :, features(j)] + jnp.concatenate(terms, axis=0)
        return block_of

    def row_squares(block):
        return lax.dot_general(
            jnp.ones((8, part), jnp.float32), block * block, (((1,), (1,)), ((), ())),
            preferred_element_type=jnp.float32, precision=lax.Precision.HIGHEST,
        )

    def squares_out(which, a, block):
        squares[which, a, me] = row_squares(block)
        for d in range(1, n):
            to_peer(
                8 + which + 4 * a, 0, squares.at[which, a, me], squares.at[which, a, me],
                lax.rem(me + d, n),
            ).start()

    def row_factor(which, a):
        all_came(8 + which + 4 * a, 0, squares.at[which, a, pl.ds(0, n - 1)])
        mean = jnp.sum(squares[which, a], axis=0) / (n * part)
        column = lax.dot_general(
            mean, jnp.full((8, 128), 0.125, jnp.float32), (((0,), (0,)), ((), ())),
            preferred_element_type=jnp.float32, precision=lax.Precision.HIGHEST,
        )
        return lax.rsqrt(column + EPSILON)

    class Gather:
        def __init__(self, a):
            self.a = a
            self.copies = []

        def send(self, phase, i, place, peer):
            there = nrm.at[place, self.a]
            copy = to_peer(phase, 2 * i + self.a, there, there, peer)
            copy.start()
            return copy

        def start(self, block):
            nrm[me, self.a] = (block * dgain_ref[:, features(me)]).astype(bf)
            for i, d in enumerate(order):
                peer = 2 * lax.rem(spot + d, half_n) + pair
                self.copies.append(self.send(6, i, me, peer))
            self.send(7, 0, me, mate)

        def forward(self):
            for i, d in enumerate(order):
                came = 2 * lax.rem(spot - d + half_n, half_n) + pair
                self.copies[i].wait_recv()
                self.send(7, 0, came, mate)

    def projections(a, r):
        all_came(7, a, nrm.at[pl.ds(0, half_n), a])
        chunk = lax.rem(a + sec, 2)
        for c in range(codes):
            x = jnp.concatenate([nrm[j, a, at_code(c), :] for j in range(n)], axis=1)
            f = r[at_code(c)]
            qs[chunk, c] = (product(x, dqkv[c, 0]) * f).astype(bf)
            kvs[chunk, 0, c] = (product(x, dqkv[c, 1]) * f).astype(bf)
            kvs[chunk, 1, c] = (product(x, dqkv[c, 2]) * f).astype(bf)
        to_partner(1 + chunk, kvs.at[chunk], kvr.at[chunk]).start()

    row_head = lax.rem(lax.broadcasted_iota(jnp.int32, (2 * lanes, lanes), 0), lanes) // DEPTH_HDIM
    col_head = lax.broadcasted_iota(jnp.int32, (2 * lanes, lanes), 1) // DEPTH_HDIM
    ones = jnp.where(row_head == col_head, 1.0, 0.0).astype(bf)
    scale = 1.0 / math.sqrt(DEPTH_HDIM)

    def scores(queries, keys):
        both = jnp.concatenate(
            [query * key.astype(jnp.float32) for query, key in zip(queries, keys)], axis=0
        )
        high = both.astype(bf)
        low = (both - high.astype(jnp.float32)).astype(bf)
        out = product(jnp.concatenate([high, low], axis=1), ones) * scale
        return [out[i * s_local:(i + 1) * s_local] for i in range(len(queries))]

    partner_swaps = [row_swap]

    def attention(a):
        queries = [qs[a, c].astype(jnp.float32) for c in range(codes)]
        pairs = [(q, k) for q in range(codes) for k in range(q + 1)]
        local = scores([queries[q] for q, _ in pairs], [kvs[a, 0, k] for _, k in pairs])
        local = dict(zip(pairs, local))
        swap = to_partner(1 + a, kvs.at[a], kvr.at[a])
        swap.wait_recv()
        partner_swaps.append(swap)
        pairs = [(q, k) for q in range(codes) for k in range(codes)]
        prior = scores([queries[q] for q, _ in pairs], [kvr[a, 0, k] for _, k in pairs])
        prior = dict(zip(pairs, prior))
        for q in range(codes):
            every = [jnp.where(sec > 0, prior[q, k], -jnp.inf) for k in range(codes)]
            every += [local[q, k] for k in range(q + 1)]
            top = every[0]
            for item in every[1:]:
                top = jnp.maximum(top, item)
            expo = [jnp.exp(item - top) for item in every]
            sums = expo[0]
            for item in expo[1:]:
                sums = sums + item
            out = None
            for k, item in enumerate(expo):
                value = kvr[a, 1, k] if k < codes else kvs[a, 1, k - codes]
                term = (item / sums).astype(bf).astype(jnp.float32) * value.astype(jnp.float32)
                out = term if out is None else out + term
            mix[a, at_code(q), :] = out.astype(bf)

    def resid_block(a):
        def block_of(j):
            return jnp.concatenate(
                [product(mix[a, at_code(c), :], dout[c, :, features(j)]) for c in range(codes)],
                axis=0,
            )
        return block_of

    def vocab_block(hidden):
        def block_of(j):
            there = pl.ds(pl.multiple_of(j * share, share), share)
            return jnp.concatenate(
                [product(hidden[at_code(c), :], headw[c, :, there]) for c in range(codes)],
                axis=0,
            )
        return block_of

    entries = [Reduction(1, a, entry_block(a), ebuf) for a in range(2)]
    entries[0].start()
    row_swap.wait_recv()
    entries[1].start()
    entries[0].forward()
    entries[1].forward()
    gathers = [Gather(a) for a in range(2)]
    for a in range(2):
        block = entries[a].result()
        squares_out(0, a, block)
        gathers[a].start(block)
        entry[lax.rem(a + sec, 2)] = block
    gathers[0].forward()
    gathers[1].forward()
    loads["dqkv"].wait()
    loads["dout"].wait()
    for a in range(2):
        factor = row_factor(0, a)
        projections(a, factor)
    resids = [Reduction(2, a, resid_block(a), dbuf) for a in range(2)]
    for a in range(2):
        attention(a)
        resids[a].start()
    resids[0].forward()
    resids[1].forward()
    loads["headw"].wait()
    heads_of = []
    for a in range(2):
        resid = entry[a] + resids[a].result()
        squares_out(1, a, resid)
        hidden = (resid * hgain_ref[:, features(me)]).astype(bf)
        heads_of.append(Reduction(5, a, vocab_block(hidden), lbuf))
        heads_of[a].start()
    heads_of[0].forward()
    factors = [row_factor(1, a) for a in range(2)]
    heads_of[1].forward()
    for a in range(2):
        out = heads_of[a].result() * factors[a][:, :1]
        logits_ref[:, a * s_local:(a + 1) * s_local, :] = out.reshape(codes, s_local, share)
    all_sent(0, tbuf.at[0])
    all_sent(1, tbuf.at[2, pl.ds(0, half_n - 1)])
    for item in entries + resids + heads_of:
        item.drain()
    all_sent(6, nrm.at[pl.ds(0, half_n - 1)])
    all_sent(7, nrm.at[pl.ds(0, half_n)])
    for which in range(2):
        for a in range(2):
            all_sent(8 + which + 4 * a, squares.at[which, a, pl.ds(0, n - 1)])
    for copy in partner_swaps:
        copy.wait_send()
    assert len(arrivals) <= recv_sem.shape[0]


def deliver_kernel(temporal_ref, logits_ref, temporal_hbm, logits_hbm, turned, sems):
    first = pltpu.make_async_copy(temporal_ref, temporal_hbm, sems.at[0])
    first.start()
    turned[...] = jnp.swapaxes(logits_ref[...], 0, 1)
    second = pltpu.make_async_copy(turned, logits_hbm, sems.at[1])
    second.start()
    first.wait()
    second.wait()


def fused(
    n, hidden_in, temporal_gain, temporal_qkv, temporal_out_weight, cache_keys, cache_values,
    lengths, depth_in, depth_embed, depth_gain, depth_qkv, depth_out_weight, head_gain,
    head_weight, tokens,
):
    s_local, width = hidden_in.shape
    codes, slim, deep = depth_in.shape
    streams = 2 * s_local
    total = codes * streams
    lanes = depth_qkv.shape[3]
    part = head_weight.shape[1]
    share = head_weight.shape[2] // n
    bf, f32 = jnp.bfloat16, jnp.float32
    pieces = 4
    big = [temporal_qkv, cache_keys, cache_values, temporal_out_weight, depth_in, depth_embed,
           depth_qkv, depth_out_weight, head_weight]
    small = [hidden_in, temporal_gain[None, :], lengths[None, :], tokens.T, depth_gain[None, :],
             head_gain[None, :]]
    vmem = pl.BlockSpec(memory_space=pltpu.VMEM)
    scratch = [pltpu.VMEM(a.shape, a.dtype) for a in small + big] + [
        pltpu.VMEM((4, n // 2, s_local, slim), bf),
        pltpu.VMEM((2, s_local, slim), bf),
        pltpu.VMEM((2, total // 2, deep), f32),
        pltpu.VMEM((4, 2, n // 2, total // 2, part), bf),
        pltpu.VMEM((n, 2, total // 2, part), bf),
        pltpu.VMEM((2, 2, codes, s_local, lanes), bf),
        pltpu.VMEM((2, 2, codes, s_local, lanes), bf),
        pltpu.VMEM((2, total // 2, lanes), bf),
        pltpu.VMEM((4, 2, n // 2, total // 2, part), bf),
        pltpu.VMEM((4, 2, n // 2, total // 2, share), bf),
        pltpu.VMEM((2, 2, n, 8, total // 2), f32),
        pltpu.VMEM((2, codes, s_local, lanes), bf),
        pltpu.VMEM((2, total // 2, part), f32),
        pltpu.SemaphoreType.DMA((3 * pieces + 14,)),
        pltpu.SemaphoreType.DMA((14,)),
        pltpu.SemaphoreType.DMA((7 * n + 4,)),
        pltpu.SemaphoreType.DMA((3,)),
        pltpu.SemaphoreType.DMA((3,)),
    ]
    temporal, logits = pl.pallas_call(
        functools.partial(tick_kernel, n, pieces),
        out_shape=(
            pltpu.VMEM((s_local, slim), bf),
            pltpu.VMEM((codes, streams, share), f32),
        ),
        in_specs=[pl.BlockSpec(memory_space=pl.ANY)] * 15,
        out_specs=(vmem, vmem),
        scratch_shapes=scratch,
        compiler_params=pltpu.CompilerParams(
            collective_id=0, has_side_effects=True, vmem_limit_bytes=60 * 1024 * 1024
        ),
    )(
        *small, *big,
    )
    return pl.pallas_call(
        deliver_kernel,
        out_shape=(
            jax.ShapeDtypeStruct((s_local, slim), bf),
            jax.ShapeDtypeStruct((streams, codes, share), f32),
        ),
        in_specs=[vmem] * 2,
        out_specs=(pl.BlockSpec(memory_space=pl.ANY),) * 2,
        scratch_shapes=[
            pltpu.VMEM((streams, codes, share), f32),
            pltpu.SemaphoreType.DMA((2,)),
        ],
        compiler_params=pltpu.CompilerParams(vmem_limit_bytes=2 * 1024 * 1024),
    )(temporal, logits)


def fits(n, arrays):
    hidden_in, depth_in, depth_qkv = arrays[0], arrays[7], arrays[10]
    total = depth_in.shape[0] * 2 * hidden_in.shape[0]
    return (
        lax.axis_size("section") == 2
        and depth_qkv.shape[3] == 128
        and arrays[13].shape[1] % 128 == 0
        and arrays[13].shape[2] % (128 * n) == 0
        and n % 2 == 0
        and total % 256 == 0
        and hidden_in.shape[0] % 16 == 0
        and arrays[4].shape[1] <= HEAD_DIM
        and arrays[2].shape[2] <= 8 * HEAD_DIM
    )


def any_size(*arrays):
    n = lax.axis_size("tp")
    if fits(n, arrays):
        return fused(n, *arrays)
    return per_device(*arrays)


def solution(mesh):
    return jax.shard_map(
        any_size,
        mesh=mesh,
        in_specs=(
            P(("grp", "section"), None),
            P(),
            P(None, None, "tp"),
            P("tp", None),
            P(("grp", "section"), None, "tp"),
            P(("grp", "section"), None, "tp"),
            P(("grp", "section")),
            P("section", "tp", None),
            P("section", "tp", None),
            P(),
            P("section", None, None, "tp"),
            P("section", "tp", None),
            P(),
            P("section", "tp", None),
            P("grp", "section"),
        ),
        out_specs=(P(("grp", "section"), "tp"), P("grp", "section", "tp")),
        check_vma=False,
    )
```

```python
import functools
import math

import jax
import jax.numpy as jnp
from jax import lax
from jax.experimental import pallas as pl
from jax.experimental.pallas import tpu as pltpu
from jax.sharding import PartitionSpec as P

HEAD_DIM = 128
DEPTH_HDIM = 64


EPSILON = 1e-05


def passed_along(block, axis, distance):
    devices = range(lax.axis_size(axis))
    route = [(i - distance, i) for i in devices if i - distance in devices]
    return lax.ppermute(block, axis, route)


def from_partner(shard, axis, distance):
    return lax.ppermute(shard, axis, [(i, i ^ 1 << distance) for i in range(lax.axis_size(axis))])


def rms_norm(values, scale):
    wide = values.astype(jnp.float32)
    return wide * lax.rsqrt(jnp.mean(wide * wide, axis=-1, keepdims=True) + EPSILON) * scale


def rotate(vectors, positions):
    halfdim = vectors.shape[-1] // 2
    spacing = jnp.arange(halfdim, dtype=jnp.float32) / halfdim
    inverse = jnp.exp(-math.log(10000.0) * spacing)
    angles = positions.astype(jnp.float32)[:, None, None] * inverse[None, None, :]
    cosine = jnp.cos(angles)
    sine = jnp.sin(angles)
    first = vectors[..., :halfdim]
    second = vectors[..., halfdim:]
    return jnp.concatenate(
        [first * cosine - second * sine, first * sine + second * cosine], axis=-1
    )


def per_device(
    hidden_in,
    temporal_gain,
    temporal_qkv,
    temporal_out_weight,
    cache_keys,
    cache_values,
    lengths,
    depth_in,
    depth_embed,
    depth_gain,
    depth_qkv,
    depth_out_weight,
    head_gain,
    head_weight,
    tokens,
):
    local_streams = hidden_in.shape[0]
    local_cols = temporal_qkv.shape[2]
    local_heads = local_cols // HEAD_DIM
    cache_len = cache_keys.shape[1]
    normed = rms_norm(hidden_in, temporal_gain).astype(jnp.bfloat16)
    projected = jnp.einsum("sd,tdf->tsf", normed, temporal_qkv, preferred_element_type=jnp.float32)
    layout = (local_streams, local_heads, HEAD_DIM)
    queries = rotate(projected[0].reshape(layout), lengths).astype(jnp.bfloat16)
    keys_new = rotate(projected[1].reshape(layout), lengths).astype(jnp.bfloat16)
    values_new = projected[2].reshape(layout).astype(jnp.bfloat16)
    cached_keys = cache_keys.reshape(local_streams, cache_len, local_heads, HEAD_DIM)
    cached_values = cache_values.reshape(local_streams, cache_len, local_heads, HEAD_DIM)
    factor = 1.0 / math.sqrt(HEAD_DIM)
    scores = (
        jnp.einsum("shd,sphd->shp", queries, cached_keys, preferred_element_type=jnp.float32)
        * factor
    )
    own_score = (
        jnp.sum(queries.astype(jnp.float32) * keys_new.astype(jnp.float32), axis=-1) * factor
    )
    valid = jnp.arange(cache_len, dtype=jnp.int32)[None, None, :] < lengths[:, None, None]
    scores = jnp.where(valid, scores, -jnp.inf)
    highest = jnp.maximum(jnp.max(scores, axis=-1), own_score)
    expo = jnp.exp(scores - highest[..., None])
    own_expo = jnp.exp(own_score - highest)
    totals = jnp.sum(expo, axis=-1) + own_expo
    weights = (expo / totals[..., None]).astype(jnp.bfloat16)
    own_weight = (own_expo / totals).astype(jnp.bfloat16)
    mixed = jnp.einsum("shp,sphd->shd", weights, cached_values, preferred_element_type=jnp.float32)
    mixed = mixed + own_weight.astype(jnp.float32)[..., None] * values_new.astype(jnp.float32)
    mixed = mixed.astype(jnp.bfloat16).reshape(local_streams, local_cols)
    partial_rows = jnp.dot(mixed, temporal_out_weight, preferred_element_type=jnp.float32)
    summed = lax.psum_scatter(partial_rows, "tp", scatter_dimension=1, tiled=True)
    slice_width = summed.shape[1]
    tp_place = lax.axis_index("tp")
    resid_in = lax.dynamic_slice_in_dim(hidden_in, tp_place * slice_width, slice_width, 1)
    temporal = (resid_in.astype(jnp.float32) + summed).astype(jnp.bfloat16)
    all_rows = lax.all_gather(temporal, "section", axis=0, tiled=True)
    streams = all_rows.shape[0]
    codes = depth_in.shape[0]
    entry_part = jnp.einsum("sd,cde->sce", all_rows, depth_in, preferred_element_type=jnp.float32)
    vocab_local = depth_embed.shape[1]
    first_id = tp_place * vocab_local
    onehot = (
        tokens[:, :, None] == first_id + jnp.arange(vocab_local, dtype=jnp.int32)[None, None, :]
    ).astype(jnp.bfloat16)
    embedded = jnp.einsum("scv,cve->sce", onehot, depth_embed, preferred_element_type=jnp.float32)
    entry_terms = entry_part + embedded
    hidden_rows = head_weight.shape[1]
    hidden_start = tp_place * hidden_rows
    entry = lax.psum(entry_terms, "tp")
    depth_normed = rms_norm(entry, depth_gain).astype(jnp.bfloat16)
    dproj = jnp.einsum(
        "sce,ctef->tscf", depth_normed, depth_qkv, preferred_element_type=jnp.float32
    ).astype(jnp.bfloat16)
    prior_keys, prior_values = passed_along((dproj[1], dproj[2]), "section", 1)
    depth_cols = dproj.shape[3]
    head_part = min(depth_cols, DEPTH_HDIM)
    local_parts = depth_cols // head_part
    sharers = DEPTH_HDIM // head_part
    all_keys = jnp.concatenate([prior_keys, dproj[1]], axis=1).reshape(
        streams, 2 * codes, local_parts, head_part
    )
    all_values = jnp.concatenate([prior_values, dproj[2]], axis=1).reshape(
        streams, 2 * codes, local_parts, head_part
    )
    depth_queries = dproj[0].reshape(streams, codes, local_parts, head_part)
    depth_scores = jnp.einsum(
        "sqhd,skhd->shqk", depth_queries, all_keys, preferred_element_type=jnp.float32
    )
    for level in range(sharers.bit_length() - 1):
        depth_scores = depth_scores + from_partner(depth_scores, "tp", level)
    depth_scores = depth_scores * (1.0 / math.sqrt(DEPTH_HDIM))
    section_place = lax.axis_index("section")
    query_pos = jnp.arange(codes, dtype=jnp.int32)[:, None]
    key_pos = jnp.arange(2 * codes, dtype=jnp.int32)[None, :]
    allowed = jnp.where(key_pos < codes, section_place > 0, key_pos - codes <= query_pos)
    depth_scores = jnp.where(allowed[None, None], depth_scores, -jnp.inf)
    depth_top = jnp.max(depth_scores, axis=-1, keepdims=True)
    depth_expo = jnp.exp(depth_scores - depth_top)
    depth_weights = (depth_expo / jnp.sum(depth_expo, axis=-1, keepdims=True)).astype(jnp.bfloat16)
    depth_mixed = jnp.einsum(
        "shqk,skhd->sqhd", depth_weights, all_values, preferred_element_type=jnp.float32
    ).astype(jnp.bfloat16)
    depth_mixed = depth_mixed.reshape(streams, codes, depth_cols)
    depth_terms = jnp.einsum(
        "scf,cfe->sce", depth_mixed, depth_out_weight, preferred_element_type=jnp.float32
    )
    resid = entry + lax.psum(depth_terms, "tp")
    head_normed = rms_norm(resid, head_gain).astype(jnp.bfloat16)
    own_hidden = lax.dynamic_slice_in_dim(head_normed, hidden_start, hidden_rows, 2)
    partial_logits = jnp.einsum(
        "sce,cev->scv", own_hidden, head_weight, preferred_element_type=jnp.float32
    )
    logits = lax.psum_scatter(partial_logits, "tp", scatter_dimension=2, tiled=True)
    return (temporal, logits)


MESH = pl.DeviceIdType.MESH


def normalised(wide, scale):
    return wide * lax.rsqrt(jnp.mean(wide * wide, axis=-1, keepdims=True) + EPSILON) * scale


def product(left, right):
    return jnp.dot(left, right, preferred_element_type=jnp.float32)


def tick_kernel(
    n, pieces,
    hidden_hbm, gain_hbm, lens_hbm, tokens_hbm, dgain_hbm, hgain_hbm,
    qkv_hbm, keys_hbm, values_hbm, outw_hbm, din_hbm, emb_hbm, dqkv_hbm, dout_hbm, headw_hbm,
    temporal_ref, logits_ref,
    hidden_ref, gain_ref, lens_ref, tokens_ref, dgain_ref, hgain_ref,
    qkv, keys, values, outw, din, emb, dqkv, dout, headw,
    tbuf, rows, ent, ebuf, nrm, kvs, kvr, mix, dbuf, lbuf, squares, qs, entry,
    load_sem, send_sem, recv_sem, pair_send, pair_recv,
):
    me = lax.axis_index("tp")
    sec = lax.axis_index("section")
    s_local, width = hidden_ref.shape
    cols = qkv.shape[2]
    heads = cols // HEAD_DIM
    cache_len = keys.shape[1]
    codes = din.shape[0]
    streams = 2 * s_local
    bf = jnp.bfloat16

    span = width // pieces
    loads = {}
    slot = 0

    def load(name, source, target):
        nonlocal slot
        loads[name] = pltpu.make_async_copy(source, target, load_sem.at[slot])
        loads[name].start()
        slot += 1

    def load_weights(t):
        for k in range(pieces):
            part = pl.ds(k * span, span)
            load(("qkv", t, k), qkv_hbm.at[t, part, :], qkv.at[t, part, :])

    load("hidden", hidden_hbm, hidden_ref)
    load("gain", gain_hbm, gain_ref)
    load("lens", lens_hbm, lens_ref)
    load_weights(0)
    load("keys", keys_hbm, keys)
    load_weights(1)
    load("values", values_hbm, values)
    load_weights(2)
    load("outw", outw_hbm, outw)
    load("tokens", tokens_hbm, tokens_ref)
    load("dgain", dgain_hbm, dgain_ref)
    load("hgain", hgain_hbm, hgain_ref)
    barrier = pltpu.get_barrier_semaphore()
    for d in range(1, n):
        pl.semaphore_signal(
            barrier, inc=1, device_id={"tp": lax.rem(me + d, n)}, device_id_type=MESH
        )
    pl.semaphore_signal(barrier, inc=1, device_id={"section": 1 - sec}, device_id_type=MESH)

    arrivals = {}

    def arrival(phase, d):
        if phase == 10:
            phase = 2
        return arrivals.setdefault((phase, d), len(arrivals))

    def to_peer(phase, d, source, target, peer):
        return pltpu.make_async_remote_copy(
            src_ref=source, dst_ref=target,
            send_sem=send_sem.at[phase], recv_sem=recv_sem.at[arrival(phase, d)],
            device_id={"tp": peer}, device_id_type=MESH,
        )

    def all_came(phase, d, there):
        to_peer(phase, d, there, there, mate).wait_recv()

    def all_sent(phase, sent):
        to_peer(phase, 0, sent, sent, mate).wait_send()

    def to_partner(phase, source, target):
        return pltpu.make_async_remote_copy(
            src_ref=source, dst_ref=target,
            send_sem=pair_send.at[phase], recv_sem=pair_recv.at[phase],
            device_id={"section": 1 - sec}, device_id_type=MESH,
        )

    half_n = n // 2
    pair = lax.rem(me, 2)
    spot = me // 2
    mate = 2 * spot + 1 - pair
    order = sorted(range(1, half_n), key=lambda d: abs(d - half_n // 2))

    def halves(size):
        return [(h, slice(h * size // 2, (h + 1) * size // 2)) for h in range(2)]

    def summed_over_tp(phase, block_of, buf):
        firsts = []
        parts = halves(buf.shape[2])
        for i, d in enumerate(order + [0]):
            target = lax.rem(spot + d, half_n)
            buf[0, i] = block_of(2 * target + 1 - pair).astype(bf)
            for h, at in parts:
                firsts.append(
                    to_peer(2 * phase, 2 * i + h, buf.at[0, i, at], buf.at[1, i, at], mate)
                )
                firsts[-1].start()
        for i, d in enumerate(order + [0]):
            target = lax.rem(spot + d, half_n)
            block = block_of(2 * target + pair)
            added = []
            for h, at in parts:
                firsts[2 * i + h].wait_recv()
                added.append(block[at] + buf[1, i, at].astype(jnp.float32))
                if d:
                    buf[2, i, at] = added[-1].astype(bf)
                    to_peer(
                        2 * phase + 1, 0, buf.at[2, i, at], buf.at[3, i, at], 2 * target + pair
                    ).start()
        return jnp.concatenate(added, axis=0)

    def finished(phase, block, buf):
        all_came(2 * phase + 1, 0, buf.at[3, pl.ds(0, half_n - 1)])
        for i in range(half_n - 1):
            block = block + buf[3, i].astype(jnp.float32)
        return block

    for name in ("hidden", "gain", "lens"):
        loads[name].wait()
    normed = normalised(hidden_ref[...].astype(jnp.float32), gain_ref[...]).astype(bf)
    half = HEAD_DIM // 2
    lane = lax.broadcasted_iota(jnp.int32, (s_local, HEAD_DIM), 1)
    spacing = lax.rem(lane, half).astype(jnp.float32) / half
    diagonal = lax.broadcasted_iota(jnp.int32, (s_local, s_local), 0) == lax.broadcasted_iota(
        jnp.int32, (s_local, s_local), 1
    )
    lens = jnp.sum(
        jnp.where(diagonal, lens_ref[...].astype(jnp.float32), 0.0), axis=1, keepdims=True
    )
    lens = jnp.broadcast_to(lens, (s_local, HEAD_DIM))
    angles = lens * jnp.exp(-math.log(10000.0) * spacing)
    cosine = jnp.cos(angles)
    sine = jnp.sin(angles)
    sine = jnp.where(lane < half, -sine, sine)

    def projected(t):
        acc = None
        for k in range(pieces):
            loads["qkv", t, k].wait()
            term = product(normed[:, k * span:(k + 1) * span], qkv[t, k * span:(k + 1) * span, :])
            acc = term if acc is None else acc + term
        if t < 2:
            turned = []
            for h in range(heads):
                one = acc[:, h * HEAD_DIM:(h + 1) * HEAD_DIM]
                turned.append(one * cosine + pltpu.roll(one, half, 1) * sine)
            acc = jnp.concatenate(turned, axis=1)
        return acc.astype(bf).astype(jnp.float32)

    factor = 1.0 / math.sqrt(HEAD_DIM)
    group = 8
    padded = 8
    owner = lax.broadcasted_iota(jnp.int32, (group, padded, cols), 2) // HEAD_DIM
    mine = owner == lax.broadcasted_iota(jnp.int32, (group, padded, cols), 1)
    place = lax.broadcasted_iota(jnp.int32, (group, padded, cache_len), 2).astype(jnp.float32)
    groups = [slice(g * group, (g + 1) * group) for g in range(s_local // group)]

    queries = projected(0)
    loads["keys"].wait()
    cached = []
    for at in groups:
        q_g = jnp.where(mine, queries[at][:, None, :], 0.0)
        cached.append(
            lax.dot_general(
                q_g.astype(bf), keys[at], (((2,), (2,)), ((0,), (0,))),
                preferred_element_type=jnp.float32,
            ) * factor
        )
    new_keys = projected(1)
    load("emb", emb_hbm, emb)
    load("din", din_hbm, din)
    load("dqkv", dqkv_hbm, dqkv)
    load("dout", dout_hbm, dout)
    load("headw", headw_hbm, headw)
    weights, own_weights = [], []
    for at, scores in zip(groups, cached):
        own_score = jnp.sum(
            jnp.where(mine, (queries[at] * new_keys[at])[:, None, :], 0.0), axis=-1, keepdims=True
        ) * factor
        live = place < lens[at, :cache_len][:, None, :]
        scores = jnp.where(live, scores, -jnp.inf)
        highest = jnp.maximum(jnp.max(scores, axis=-1, keepdims=True), own_score)
        expo = jnp.exp(scores - highest)
        own_expo = jnp.exp(own_score - highest)
        totals = jnp.sum(expo, axis=-1, keepdims=True) + own_expo
        weights.append((expo / totals).astype(bf))
        own_weight = (own_expo / totals).astype(bf).astype(jnp.float32)
        own_weights.append(jnp.sum(jnp.where(mine, own_weight, 0.0), axis=1))
    loads["values"].wait()
    mixed = []
    for at, weight in zip(groups, weights):
        out = lax.dot_general(
            weight, values[at], (((2,), (1,)), ((0,), (0,))), preferred_element_type=jnp.float32
        )
        mixed.append(jnp.sum(jnp.where(mine, out, 0.0), axis=1))
    mixed = jnp.concatenate(mixed, axis=0)
    own_weights = jnp.concatenate(own_weights, axis=0)
    mixed = (mixed + own_weights * projected(2)).astype(bf)

    loads["outw"].wait()
    slim = width // n
    pl.semaphore_wait(barrier, n)

    def row_block(j):
        return product(mixed, outw[:, pl.ds(pl.multiple_of(j * slim, slim), slim)])

    summed = summed_over_tp(0, row_block, tbuf)

    vocab = emb.shape[1]
    for name in ("emb", "tokens", "dgain", "hgain"):
        loads[name].wait()
    ids = lax.broadcasted_iota(jnp.int32, (vocab, streams), 0) + me * vocab
    for c in range(codes):
        onehot = jnp.where(tokens_ref[c:c + 1, :] == ids, 1.0, 0.0).astype(bf)
        looked_up = lax.dot_general(
            onehot, emb[c], (((0,), (0,)), ((), ())), preferred_element_type=jnp.float32
        )
        for a in range(2):
            ent[lax.rem(a + sec, 2), c * s_local:(c + 1) * s_local, :] = looked_up[
                a * s_local:(a + 1) * s_local
            ]
    loads["din"].wait()

    summed = finished(0, summed, tbuf)
    start = pl.multiple_of(me * slim, slim)
    temporal = (hidden_ref[:, pl.ds(start, slim)].astype(jnp.float32) + summed).astype(bf)
    temporal_ref[...] = temporal
    rows[0] = temporal
    row_swap = to_partner(0, rows.at[0], rows.at[1])
    row_swap.start()

    part = din.shape[2] // n
    share = headw.shape[2] // n
    lanes = dqkv.shape[3]

    def at_code(c):
        return slice(c * s_local, (c + 1) * s_local)

    def features(j):
        return pl.ds(pl.multiple_of(j * part, part), part)

    turns = order + [0]

    class Reduction:
        def __init__(self, phase, a, block_of, buf):
            self.phase, self.a, self.block_of, self.buf = phase, a, block_of, buf
            self.firsts = {}

        def send(self, stage, i, h, at, peer):
            spot_of = (self.a, i, at)
            copy = to_peer(
                2 * self.phase + stage, self.a if stage else 4 * i + 2 * h + self.a,
                self.buf.at[(2 * stage, *spot_of)], self.buf.at[(2 * stage + 1, *spot_of)], peer,
            )
            copy.start()
            return copy

        def start_one(self, i):
            target = lax.rem(spot + turns[i], half_n)
            self.buf[0, self.a, i] = self.block_of(2 * target + 1 - pair).astype(bf)
            for h, at in halves(self.buf.shape[3]):
                self.firsts[i, h] = self.send(0, i, h, at, mate)

        def forward_one(self, i):
            target = lax.rem(spot + turns[i], half_n)
            block = self.block_of(2 * target + pair)
            added = []
            for h, at in halves(self.buf.shape[3]):
                self.firsts[i, h].wait_recv()
                added.append(block[at] + self.buf[1, self.a, i, at].astype(jnp.float32))
                if turns[i]:
                    self.buf[2, self.a, i, at] = added[-1].astype(bf)
                    self.send(1, i, h, at, 2 * target + pair)
            self.own = jnp.concatenate(added, axis=0)

        def start(self):
            for i in range(half_n):
                self.start_one(i)

        def forward(self):
            for i in range(half_n):
                self.forward_one(i)

        def result(self):
            block = self.own
            all_came(2 * self.phase + 1, self.a, self.buf.at[3, self.a, pl.ds(0, half_n - 1)])
            for i in range(half_n - 1):
                block = block + self.buf[3, self.a, i].astype(jnp.float32)
            return block

        def drain(self):
            all_sent(2 * self.phase, self.buf.at[0, self.a])
            all_sent(2 * self.phase + 1, self.buf.at[2, self.a, pl.ds(0, half_n - 1)])

    def entry_block(a):
        def block_of(j):
            terms = [product(rows[a], din[c, :, features(j)]) for c in range(codes)]
            return ent[a, :, features(j)] + jnp.concatenate(terms, axis=0)
        return block_of

    def row_squares(block):
        return lax.dot_general(
            jnp.ones((8, part), jnp.float32), block * block, (((1,), (1,)), ((), ())),
            preferred_element_type=jnp.float32, precision=lax.Precision.HIGHEST,
        )

    def squares_out(which, a, block):
        squares[which, a, me] = row_squares(block)
        for d in range(1, n):
            to_peer(
                8 + which + 4 * a, 0, squares.at[which, a, me], squares.at[which, a, me],
                lax.rem(me + d, n),
            ).start()

    def row_factor(which, a):
        all_came(8 + which + 4 * a, 0, squares.at[which, a, pl.ds(0, n - 1)])
        mean = jnp.sum(squares[which, a], axis=0) / (n * part)
        column = lax.dot_general(
            mean, jnp.full((8, 128), 0.125, jnp.float32), (((0,), (0,)), ((), ())),
            preferred_element_type=jnp.float32, precision=lax.Precision.HIGHEST,
        )
        return lax.rsqrt(column + EPSILON)

    class Gather:
        def __init__(self, a):
            self.a = a
            self.copies = []

        def send(self, phase, i, place, peer):
            there = nrm.at[place, self.a]
            copy = to_peer(phase, 2 * i + self.a, there, there, peer)
            copy.start()
            return copy

        def start(self, block):
            nrm[me, self.a] = (block * dgain_ref[:, features(me)]).astype(bf)
            for i, d in enumerate(order):
                peer = 2 * lax.rem(spot + d, half_n) + pair
                self.copies.append(self.send(6, i, me, peer))
            self.send(7, 0, me, mate)

        def forward_one(self, i):
            came = 2 * lax.rem(spot - order[i] + half_n, half_n) + pair
            self.copies[i].wait_recv()
            self.send(7, 0, came, mate)

        def forward(self):
            for i in range(half_n - 1):
                self.forward_one(i)

    def projections(a, r):
        all_came(7, a, nrm.at[pl.ds(0, half_n), a])
        chunk = lax.rem(a + sec, 2)
        for c in range(codes):
            x = jnp.concatenate([nrm[j, a, at_code(c), :] for j in range(n)], axis=1)
            f = r[at_code(c)]
            qs[chunk, c] = (product(x, dqkv[c, 0]) * f).astype(bf)
            kvs[chunk, 0, c] = (product(x, dqkv[c, 1]) * f).astype(bf)
            kvs[chunk, 1, c] = (product(x, dqkv[c, 2]) * f).astype(bf)
        to_partner(1 + chunk, kvs.at[chunk], kvr.at[chunk]).start()

    row_head = lax.rem(lax.broadcasted_iota(jnp.int32, (2 * lanes, lanes), 0), lanes) // DEPTH_HDIM
    col_head = lax.broadcasted_iota(jnp.int32, (2 * lanes, lanes), 1) // DEPTH_HDIM
    ones = jnp.where(row_head == col_head, 1.0, 0.0).astype(bf)
    scale = 1.0 / math.sqrt(DEPTH_HDIM)

    def scores(queries, keys):
        both = jnp.concatenate(
            [query * key.astype(jnp.float32) for query, key in zip(queries, keys)], axis=0
        )
        high = both.astype(bf)
        low = (both - high.astype(jnp.float32)).astype(bf)
        out = product(jnp.concatenate([high, low], axis=1), ones) * scale
        return [out[i * s_local:(i + 1) * s_local] for i in range(len(queries))]

    partner_swaps = [row_swap]

    def attention(a):
        queries = [qs[a, c].astype(jnp.float32) for c in range(codes)]
        pairs = [(q, k) for q in range(codes) for k in range(q + 1)]
        local = scores([queries[q] for q, _ in pairs], [kvs[a, 0, k] for _, k in pairs])
        local = dict(zip(pairs, local))
        swap = to_partner(1 + a, kvs.at[a], kvr.at[a])
        swap.wait_recv()
        partner_swaps.append(swap)
        pairs = [(q, k) for q in range(codes) for k in range(codes)]
        prior = scores([queries[q] for q, _ in pairs], [kvr[a, 0, k] for _, k in pairs])
        prior = dict(zip(pairs, prior))
        for q in range(codes):
            every = [jnp.where(sec > 0, prior[q, k], -jnp.inf) for k in range(codes)]
            every += [local[q, k] for k in range(q + 1)]
            top = every[0]
            for item in every[1:]:
                top = jnp.maximum(top, item)
            expo = [jnp.exp(item - top) for item in every]
            sums = expo[0]
            for item in expo[1:]:
                sums = sums + item
            out = None
            for k, item in enumerate(expo):
                value = kvr[a, 1, k] if k < codes else kvs[a, 1, k - codes]
                term = (item / sums).astype(bf).astype(jnp.float32) * value.astype(jnp.float32)
                out = term if out is None else out + term
            mix[a, at_code(q), :] = out.astype(bf)

    def resid_block(a):
        def block_of(j):
            return jnp.concatenate(
                [product(mix[a, at_code(c), :], dout[c, :, features(j)]) for c in range(codes)],
                axis=0,
            )
        return block_of

    def vocab_block(hidden):
        def block_of(j):
            there = pl.ds(pl.multiple_of(j * share, share), share)
            return jnp.concatenate(
                [product(hidden[at_code(c), :], headw[c, :, there]) for c in range(codes)],
                axis=0,
            )
        return block_of

    entries = [Reduction(1, a, entry_block(a), ebuf) for a in range(2)]
    entries[0].start()
    row_swap.wait_recv()
    for i in range(half_n):
        entries[1].start_one(i)
        if i:
            entries[0].forward_one(i - 1)
    entries[0].forward_one(half_n - 1)
    entries[1].forward()
    gathers = [Gather(a) for a in range(2)]
    for a in range(2):
        block = entries[a].result()
        gathers[a].start(block)
        squares_out(0, a, block)
        entry[lax.rem(a + sec, 2)] = block
    gathers[0].forward()
    for i in range(half_n - 1):
        if i == half_n - 2:
            factor = row_factor(0, 0)
        gathers[1].forward_one(i)
    loads["dqkv"].wait()
    loads["dout"].wait()
    for a in range(2):
        if a:
            factor = row_factor(0, a)
        projections(a, factor)
    resids = [Reduction(2, a, resid_block(a), dbuf) for a in range(2)]
    for a in range(2):
        attention(a)
        resids[a].start()
    resids[0].forward()
    resids[1].forward()
    loads["headw"].wait()
    heads_of = []
    for a in range(2):
        resid = entry[a] + resids[a].result()
        if a:
            squares_out(1, a, resid)
        hidden = (resid * hgain_ref[:, features(me)]).astype(bf)
        heads_of.append(Reduction(5, a, vocab_block(hidden), lbuf))
        heads_of[a].start()
        if not a:
            squares_out(1, a, resid)
    heads_of[0].forward()
    heads_of[1].forward()
    factors = [row_factor(1, a) for a in range(2)]
    for a in range(2):
        out = heads_of[a].result() * factors[a][:, :1]
        logits_ref[:, a * s_local:(a + 1) * s_local, :] = out.reshape(codes, s_local, share)
    all_sent(0, tbuf.at[0])
    all_sent(1, tbuf.at[2, pl.ds(0, half_n - 1)])
    for item in entries + resids + heads_of:
        item.drain()
    all_sent(6, nrm.at[pl.ds(0, half_n - 1)])
    all_sent(7, nrm.at[pl.ds(0, half_n)])
    for which in range(2):
        for a in range(2):
            all_sent(8 + which + 4 * a, squares.at[which, a, pl.ds(0, n - 1)])
    for copy in partner_swaps:
        copy.wait_send()
    assert len(arrivals) <= recv_sem.shape[0]


def deliver_kernel(temporal_ref, logits_ref, temporal_hbm, logits_hbm, turned, sems):
    first = pltpu.make_async_copy(temporal_ref, temporal_hbm, sems.at[0])
    first.start()
    turned[...] = jnp.swapaxes(logits_ref[...], 0, 1)
    second = pltpu.make_async_copy(turned, logits_hbm, sems.at[1])
    second.start()
    first.wait()
    second.wait()


def fused(
    n, hidden_in, temporal_gain, temporal_qkv, temporal_out_weight, cache_keys, cache_values,
    lengths, depth_in, depth_embed, depth_gain, depth_qkv, depth_out_weight, head_gain,
    head_weight, tokens,
):
    s_local, width = hidden_in.shape
    codes, slim, deep = depth_in.shape
    streams = 2 * s_local
    total = codes * streams
    lanes = depth_qkv.shape[3]
    part = head_weight.shape[1]
    share = head_weight.shape[2] // n
    bf, f32 = jnp.bfloat16, jnp.float32
    pieces = 4
    big = [temporal_qkv, cache_keys, cache_values, temporal_out_weight, depth_in, depth_embed,
           depth_qkv, depth_out_weight, head_weight]
    small = [hidden_in, temporal_gain[None, :], lengths[None, :], tokens.T, depth_gain[None, :],
             head_gain[None, :]]
    vmem = pl.BlockSpec(memory_space=pltpu.VMEM)
    scratch = [pltpu.VMEM(a.shape, a.dtype) for a in small + big] + [
        pltpu.VMEM((4, n // 2, s_local, slim), bf),
        pltpu.VMEM((2, s_local, slim), bf),
        pltpu.VMEM((2, total // 2, deep), f32),
        pltpu.VMEM((4, 2, n // 2, total // 2, part), bf),
        pltpu.VMEM((n, 2, total // 2, part), bf),
        pltpu.VMEM((2, 2, codes, s_local, lanes), bf),
        pltpu.VMEM((2, 2, codes, s_local, lanes), bf),
        pltpu.VMEM((2, total // 2, lanes), bf),
        pltpu.VMEM((4, 2, n // 2, total // 2, part), bf),
        pltpu.VMEM((4, 2, n // 2, total // 2, share), bf),
        pltpu.VMEM((2, 2, n, 8, total // 2), f32),
        pltpu.VMEM((2, codes, s_local, lanes), bf),
        pltpu.VMEM((2, total // 2, part), f32),
        pltpu.SemaphoreType.DMA((3 * pieces + 14,)),
        pltpu.SemaphoreType.DMA((14,)),
        pltpu.SemaphoreType.DMA((7 * n + 4,)),
        pltpu.SemaphoreType.DMA((3,)),
        pltpu.SemaphoreType.DMA((3,)),
    ]
    temporal, logits = pl.pallas_call(
        functools.partial(tick_kernel, n, pieces),
        out_shape=(
            pltpu.VMEM((s_local, slim), bf),
            pltpu.VMEM((codes, streams, share), f32),
        ),
        in_specs=[pl.BlockSpec(memory_space=pl.ANY)] * 15,
        out_specs=(vmem, vmem),
        scratch_shapes=scratch,
        compiler_params=pltpu.CompilerParams(
            collective_id=0, has_side_effects=True, vmem_limit_bytes=60 * 1024 * 1024
        ),
    )(
        *small, *big,
    )
    return pl.pallas_call(
        deliver_kernel,
        out_shape=(
            jax.ShapeDtypeStruct((s_local, slim), bf),
            jax.ShapeDtypeStruct((streams, codes, share), f32),
        ),
        in_specs=[vmem] * 2,
        out_specs=(pl.BlockSpec(memory_space=pl.ANY),) * 2,
        scratch_shapes=[
            pltpu.VMEM((streams, codes, share), f32),
            pltpu.SemaphoreType.DMA((2,)),
        ],
        compiler_params=pltpu.CompilerParams(vmem_limit_bytes=2 * 1024 * 1024),
    )(temporal, logits)


def fits(n, arrays):
    hidden_in, depth_in, depth_qkv = arrays[0], arrays[7], arrays[10]
    total = depth_in.shape[0] * 2 * hidden_in.shape[0]
    return (
        lax.axis_size("section") == 2
        and depth_qkv.shape[3] == 128
        and arrays[13].shape[1] % 128 == 0
        and arrays[13].shape[2] % (128 * n) == 0
        and n % 2 == 0
        and total % 256 == 0
        and hidden_in.shape[0] % 16 == 0
        and arrays[4].shape[1] <= HEAD_DIM
        and arrays[2].shape[2] <= 8 * HEAD_DIM
    )


def any_size(*arrays):
    n = lax.axis_size("tp")
    if fits(n, arrays):
        return fused(n, *arrays)
    return per_device(*arrays)


def solution(mesh):
    return jax.shard_map(
        any_size,
        mesh=mesh,
        in_specs=(
            P(("grp", "section"), None),
            P(),
            P(None, None, "tp"),
            P("tp", None),
            P(("grp", "section"), None, "tp"),
            P(("grp", "section"), None, "tp"),
            P(("grp", "section")),
            P("section", "tp", None),
            P("section", "tp", None),
            P(),
            P("section", None, None, "tp"),
            P("section", "tp", None),
            P(),
            P("section", "tp", None),
            P("grp", "section"),
        ),
        out_specs=(P(("grp", "section"), "tp"), P("grp", "section", "tp")),
        check_vma=False,
    )
```

```python
import functools
import math

import jax
import jax.numpy as jnp
from jax import lax
from jax.experimental import pallas as pl
from jax.experimental.pallas import tpu as pltpu
from jax.sharding import PartitionSpec as P

HEAD_DIM = 128
DEPTH_HDIM = 64


EPSILON = 1e-05


def passed_along(block, axis, distance):
    devices = range(lax.axis_size(axis))
    route = [(i - distance, i) for i in devices if i - distance in devices]
    return lax.ppermute(block, axis, route)


def from_partner(shard, axis, distance):
    return lax.ppermute(shard, axis, [(i, i ^ 1 << distance) for i in range(lax.axis_size(axis))])


def rms_norm(values, scale):
    wide = values.astype(jnp.float32)
    return wide * lax.rsqrt(jnp.mean(wide * wide, axis=-1, keepdims=True) + EPSILON) * scale


def rotate(vectors, positions):
    halfdim = vectors.shape[-1] // 2
    spacing = jnp.arange(halfdim, dtype=jnp.float32) / halfdim
    inverse = jnp.exp(-math.log(10000.0) * spacing)
    angles = positions.astype(jnp.float32)[:, None, None] * inverse[None, None, :]
    cosine = jnp.cos(angles)
    sine = jnp.sin(angles)
    first = vectors[..., :halfdim]
    second = vectors[..., halfdim:]
    return jnp.concatenate(
        [first * cosine - second * sine, first * sine + second * cosine], axis=-1
    )


def per_device(
    hidden_in,
    temporal_gain,
    temporal_qkv,
    temporal_out_weight,
    cache_keys,
    cache_values,
    lengths,
    depth_in,
    depth_embed,
    depth_gain,
    depth_qkv,
    depth_out_weight,
    head_gain,
    head_weight,
    tokens,
):
    local_streams = hidden_in.shape[0]
    local_cols = temporal_qkv.shape[2]
    local_heads = local_cols // HEAD_DIM
    cache_len = cache_keys.shape[1]
    normed = rms_norm(hidden_in, temporal_gain).astype(jnp.bfloat16)
    projected = jnp.einsum("sd,tdf->tsf", normed, temporal_qkv, preferred_element_type=jnp.float32)
    layout = (local_streams, local_heads, HEAD_DIM)
    queries = rotate(projected[0].reshape(layout), lengths).astype(jnp.bfloat16)
    keys_new = rotate(projected[1].reshape(layout), lengths).astype(jnp.bfloat16)
    values_new = projected[2].reshape(layout).astype(jnp.bfloat16)
    cached_keys = cache_keys.reshape(local_streams, cache_len, local_heads, HEAD_DIM)
    cached_values = cache_values.reshape(local_streams, cache_len, local_heads, HEAD_DIM)
    factor = 1.0 / math.sqrt(HEAD_DIM)
    scores = (
        jnp.einsum("shd,sphd->shp", queries, cached_keys, preferred_element_type=jnp.float32)
        * factor
    )
    own_score = (
        jnp.sum(queries.astype(jnp.float32) * keys_new.astype(jnp.float32), axis=-1) * factor
    )
    valid = jnp.arange(cache_len, dtype=jnp.int32)[None, None, :] < lengths[:, None, None]
    scores = jnp.where(valid, scores, -jnp.inf)
    highest = jnp.maximum(jnp.max(scores, axis=-1), own_score)
    expo = jnp.exp(scores - highest[..., None])
    own_expo = jnp.exp(own_score - highest)
    totals = jnp.sum(expo, axis=-1) + own_expo
    weights = (expo / totals[..., None]).astype(jnp.bfloat16)
    own_weight = (own_expo / totals).astype(jnp.bfloat16)
    mixed = jnp.einsum("shp,sphd->shd", weights, cached_values, preferred_element_type=jnp.float32)
    mixed = mixed + own_weight.astype(jnp.float32)[..., None] * values_new.astype(jnp.float32)
    mixed = mixed.astype(jnp.bfloat16).reshape(local_streams, local_cols)
    partial_rows = jnp.dot(mixed, temporal_out_weight, preferred_element_type=jnp.float32)
    summed = lax.psum_scatter(partial_rows, "tp", scatter_dimension=1, tiled=True)
    slice_width = summed.shape[1]
    tp_place = lax.axis_index("tp")
    resid_in = lax.dynamic_slice_in_dim(hidden_in, tp_place * slice_width, slice_width, 1)
    temporal = (resid_in.astype(jnp.float32) + summed).astype(jnp.bfloat16)
    all_rows = lax.all_gather(temporal, "section", axis=0, tiled=True)
    streams = all_rows.shape[0]
    codes = depth_in.shape[0]
    entry_part = jnp.einsum("sd,cde->sce", all_rows, depth_in, preferred_element_type=jnp.float32)
    vocab_local = depth_embed.shape[1]
    first_id = tp_place * vocab_local
    onehot = (
        tokens[:, :, None] == first_id + jnp.arange(vocab_local, dtype=jnp.int32)[None, None, :]
    ).astype(jnp.bfloat16)
    embedded = jnp.einsum("scv,cve->sce", onehot, depth_embed, preferred_element_type=jnp.float32)
    entry_terms = entry_part + embedded
    hidden_rows = head_weight.shape[1]
    hidden_start = tp_place * hidden_rows
    entry = lax.psum(entry_terms, "tp")
    depth_normed = rms_norm(entry, depth_gain).astype(jnp.bfloat16)
    dproj = jnp.einsum(
        "sce,ctef->tscf", depth_normed, depth_qkv, preferred_element_type=jnp.float32
    ).astype(jnp.bfloat16)
    prior_keys, prior_values = passed_along((dproj[1], dproj[2]), "section", 1)
    depth_cols = dproj.shape[3]
    head_part = min(depth_cols, DEPTH_HDIM)
    local_parts = depth_cols // head_part
    sharers = DEPTH_HDIM // head_part
    all_keys = jnp.concatenate([prior_keys, dproj[1]], axis=1).reshape(
        streams, 2 * codes, local_parts, head_part
    )
    all_values = jnp.concatenate([prior_values, dproj[2]], axis=1).reshape(
        streams, 2 * codes, local_parts, head_part
    )
    depth_queries = dproj[0].reshape(streams, codes, local_parts, head_part)
    depth_scores = jnp.einsum(
        "sqhd,skhd->shqk", depth_queries, all_keys, preferred_element_type=jnp.float32
    )
    for level in range(sharers.bit_length() - 1):
        depth_scores = depth_scores + from_partner(depth_scores, "tp", level)
    depth_scores = depth_scores * (1.0 / math.sqrt(DEPTH_HDIM))
    section_place = lax.axis_index("section")
    query_pos = jnp.arange(codes, dtype=jnp.int32)[:, None]
    key_pos = jnp.arange(2 * codes, dtype=jnp.int32)[None, :]
    allowed = jnp.where(key_pos < codes, section_place > 0, key_pos - codes <= query_pos)
    depth_scores = jnp.where(allowed[None, None], depth_scores, -jnp.inf)
    depth_top = jnp.max(depth_scores, axis=-1, keepdims=True)
    depth_expo = jnp.exp(depth_scores - depth_top)
    depth_weights = (depth_expo / jnp.sum(depth_expo, axis=-1, keepdims=True)).astype(jnp.bfloat16)
    depth_mixed = jnp.einsum(
        "shqk,skhd->sqhd", depth_weights, all_values, preferred_element_type=jnp.float32
    ).astype(jnp.bfloat16)
    depth_mixed = depth_mixed.reshape(streams, codes, depth_cols)
    depth_terms = jnp.einsum(
        "scf,cfe->sce", depth_mixed, depth_out_weight, preferred_element_type=jnp.float32
    )
    resid = entry + lax.psum(depth_terms, "tp")
    head_normed = rms_norm(resid, head_gain).astype(jnp.bfloat16)
    own_hidden = lax.dynamic_slice_in_dim(head_normed, hidden_start, hidden_rows, 2)
    partial_logits = jnp.einsum(
        "sce,cev->scv", own_hidden, head_weight, preferred_element_type=jnp.float32
    )
    logits = lax.psum_scatter(partial_logits, "tp", scatter_dimension=2, tiled=True)
    return (temporal, logits)


MESH = pl.DeviceIdType.MESH


def normalised(wide, scale):
    return wide * lax.rsqrt(jnp.mean(wide * wide, axis=-1, keepdims=True) + EPSILON) * scale


def product(left, right):
    return jnp.dot(left, right, preferred_element_type=jnp.float32)


def tick_kernel(
    n, pieces,
    hidden_hbm, gain_hbm, lens_hbm, tokens_hbm, dgain_hbm, hgain_hbm,
    qkv_hbm, keys_hbm, values_hbm, outw_hbm, din_hbm, emb_hbm, dqkv_hbm, dout_hbm, headw_hbm,
    temporal_ref, logits_ref,
    hidden_ref, gain_ref, lens_ref, tokens_ref, dgain_ref, hgain_ref,
    qkv, keys, values, outw, din, emb, dqkv, dout, headw,
    tbuf, rows, ent, ebuf, nrm, kvs, kvr, mix, dbuf, lbuf, squares, qs, entry,
    load_sem, send_sem, recv_sem, pair_send, pair_recv,
):
    me = lax.axis_index("tp")
    sec = lax.axis_index("section")
    s_local, width = hidden_ref.shape
    cols = qkv.shape[2]
    heads = cols // HEAD_DIM
    cache_len = keys.shape[1]
    codes = din.shape[0]
    streams = 2 * s_local
    bf = jnp.bfloat16

    span = width // pieces
    loads = {}
    slot = 0

    def load(name, source, target):
        nonlocal slot
        loads[name] = pltpu.make_async_copy(source, target, load_sem.at[slot])
        loads[name].start()
        slot += 1

    half_n = n // 2
    pair = lax.rem(me, 2)
    spot = me // 2
    mate = 2 * spot + 1 - pair
    order = sorted(range(1, half_n), key=lambda d: abs(d - half_n // 2))
    slim = width // n

    def row_columns(j):
        return pl.ds(pl.multiple_of(j * slim, slim), slim)

    def load_weights(t):
        for k in range(pieces):
            part = pl.ds(k * span, span)
            load(("qkv", t, k), qkv_hbm.at[t, part, :], qkv.at[t, part, :])

    load("hidden", hidden_hbm, hidden_ref)
    load("gain", gain_hbm, gain_ref)
    load("lens", lens_hbm, lens_ref)
    load_weights(0)
    load("keys", keys_hbm, keys)
    load_weights(1)
    load("values", values_hbm, values)
    load_weights(2)
    for step in range(n):
        target = 2 * lax.rem(spot + (order + [0])[step % half_n], half_n)
        at = row_columns(target + (1 - pair if step < half_n else pair))
        load(("outw", step), outw_hbm.at[:, at], outw.at[:, at])
    load("tokens", tokens_hbm, tokens_ref)
    load("dgain", dgain_hbm, dgain_ref)
    load("hgain", hgain_hbm, hgain_ref)
    barrier = pltpu.get_barrier_semaphore()
    for d in range(1, n):
        pl.semaphore_signal(
            barrier, inc=1, device_id={"tp": lax.rem(me + d, n)}, device_id_type=MESH
        )
    pl.semaphore_signal(barrier, inc=1, device_id={"section": 1 - sec}, device_id_type=MESH)

    arrivals = {}

    def arrival(phase, d):
        if phase == 10:
            phase = 2
        return arrivals.setdefault((phase, d), len(arrivals))

    def to_peer(phase, d, source, target, peer):
        return pltpu.make_async_remote_copy(
            src_ref=source, dst_ref=target,
            send_sem=send_sem.at[phase], recv_sem=recv_sem.at[arrival(phase, d)],
            device_id={"tp": peer}, device_id_type=MESH,
        )

    def all_came(phase, d, there):
        to_peer(phase, d, there, there, mate).wait_recv()

    def all_sent(phase, sent):
        to_peer(phase, 0, sent, sent, mate).wait_send()

    def to_partner(phase, source, target):
        return pltpu.make_async_remote_copy(
            src_ref=source, dst_ref=target,
            send_sem=pair_send.at[phase], recv_sem=pair_recv.at[phase],
            device_id={"section": 1 - sec}, device_id_type=MESH,
        )

    def halves(size):
        return [(h, slice(h * size // 2, (h + 1) * size // 2)) for h in range(2)]

    def summed_over_tp(phase, block_of, buf):
        firsts = []
        parts = halves(buf.shape[2])
        for i, d in enumerate(order + [0]):
            target = lax.rem(spot + d, half_n)
            buf[0, i] = block_of(2 * target + 1 - pair).astype(bf)
            for h, at in parts:
                firsts.append(
                    to_peer(2 * phase, 2 * i + h, buf.at[0, i, at], buf.at[1, i, at], mate)
                )
                firsts[-1].start()
        for i, d in enumerate(order + [0]):
            target = lax.rem(spot + d, half_n)
            block = block_of(2 * target + pair)
            added = []
            for h, at in parts:
                firsts[2 * i + h].wait_recv()
                added.append(block[at] + buf[1, i, at].astype(jnp.float32))
                if d:
                    buf[2, i, at] = added[-1].astype(bf)
                    to_peer(
                        2 * phase + 1, 0, buf.at[2, i, at], buf.at[3, i, at], 2 * target + pair
                    ).start()
        return jnp.concatenate(added, axis=0)

    def finished(phase, block, buf):
        all_came(2 * phase + 1, 0, buf.at[3, pl.ds(0, half_n - 1)])
        for i in range(half_n - 1):
            block = block + buf[3, i].astype(jnp.float32)
        return block

    for name in ("hidden", "gain", "lens"):
        loads[name].wait()
    normed = normalised(hidden_ref[...].astype(jnp.float32), gain_ref[...]).astype(bf)
    half = HEAD_DIM // 2
    lane = lax.broadcasted_iota(jnp.int32, (s_local, HEAD_DIM), 1)
    spacing = lax.rem(lane, half).astype(jnp.float32) / half
    diagonal = lax.broadcasted_iota(jnp.int32, (s_local, s_local), 0) == lax.broadcasted_iota(
        jnp.int32, (s_local, s_local), 1
    )
    lens = jnp.sum(
        jnp.where(diagonal, lens_ref[...].astype(jnp.float32), 0.0), axis=1, keepdims=True
    )
    lens = jnp.broadcast_to(lens, (s_local, HEAD_DIM))
    angles = lens * jnp.exp(-math.log(10000.0) * spacing)
    cosine = jnp.cos(angles)
    sine = jnp.sin(angles)
    sine = jnp.where(lane < half, -sine, sine)

    def projected(t):
        acc = None
        for k in range(pieces):
            loads["qkv", t, k].wait()
            term = product(normed[:, k * span:(k + 1) * span], qkv[t, k * span:(k + 1) * span, :])
            acc = term if acc is None else acc + term
        if t < 2:
            turned = []
            for h in range(heads):
                one = acc[:, h * HEAD_DIM:(h + 1) * HEAD_DIM]
                turned.append(one * cosine + pltpu.roll(one, half, 1) * sine)
            acc = jnp.concatenate(turned, axis=1)
        return acc.astype(bf).astype(jnp.float32)

    factor = 1.0 / math.sqrt(HEAD_DIM)
    group = 8
    padded = 8
    owner = lax.broadcasted_iota(jnp.int32, (group, padded, cols), 2) // HEAD_DIM
    mine = owner == lax.broadcasted_iota(jnp.int32, (group, padded, cols), 1)
    place = lax.broadcasted_iota(jnp.int32, (group, padded, cache_len), 2).astype(jnp.float32)
    groups = [slice(g * group, (g + 1) * group) for g in range(s_local // group)]

    queries = projected(0)
    loads["keys"].wait()
    cached = []
    for at in groups:
        q_g = jnp.where(mine, queries[at][:, None, :], 0.0)
        cached.append(
            lax.dot_general(
                q_g.astype(bf), keys[at], (((2,), (2,)), ((0,), (0,))),
                preferred_element_type=jnp.float32,
            ) * factor
        )
    new_keys = projected(1)
    load("emb", emb_hbm, emb)
    load("din", din_hbm, din)
    load("dqkv", dqkv_hbm, dqkv)
    load("dout", dout_hbm, dout)
    load("headw", headw_hbm, headw)
    weights, own_weights = [], []
    for at, scores in zip(groups, cached):
        own_score = jnp.sum(
            jnp.where(mine, (queries[at] * new_keys[at])[:, None, :], 0.0), axis=-1, keepdims=True
        ) * factor
        live = place < lens[at, :cache_len][:, None, :]
        scores = jnp.where(live, scores, -jnp.inf)
        highest = jnp.maximum(jnp.max(scores, axis=-1, keepdims=True), own_score)
        expo = jnp.exp(scores - highest)
        own_expo = jnp.exp(own_score - highest)
        totals = jnp.sum(expo, axis=-1, keepdims=True) + own_expo
        weights.append((expo / totals).astype(bf))
        own_weight = (own_expo / totals).astype(bf).astype(jnp.float32)
        own_weights.append(jnp.sum(jnp.where(mine, own_weight, 0.0), axis=1))
    loads["values"].wait()
    mixed = []
    for at, weight in zip(groups, weights):
        out = lax.dot_general(
            weight, values[at], (((2,), (1,)), ((0,), (0,))), preferred_element_type=jnp.float32
        )
        mixed.append(jnp.sum(jnp.where(mine, out, 0.0), axis=1))
    mixed = jnp.concatenate(mixed, axis=0)
    own_weights = jnp.concatenate(own_weights, axis=0)
    mixed = (mixed + own_weights * projected(2)).astype(bf)

    steps = iter(range(n))
    pl.semaphore_wait(barrier, n)

    def row_block(j):
        loads["outw", next(steps)].wait()
        return product(mixed, outw[:, row_columns(j)])

    summed = summed_over_tp(0, row_block, tbuf)

    vocab = emb.shape[1]
    for name in ("emb", "tokens", "dgain", "hgain"):
        loads[name].wait()
    ids = lax.broadcasted_iota(jnp.int32, (vocab, streams), 0) + me * vocab
    for c in range(codes):
        onehot = jnp.where(tokens_ref[c:c + 1, :] == ids, 1.0, 0.0).astype(bf)
        looked_up = lax.dot_general(
            onehot, emb[c], (((0,), (0,)), ((), ())), preferred_element_type=jnp.float32
        )
        for a in range(2):
            ent[lax.rem(a + sec, 2), c * s_local:(c + 1) * s_local, :] = looked_up[
                a * s_local:(a + 1) * s_local
            ]
    loads["din"].wait()

    summed = finished(0, summed, tbuf)
    start = pl.multiple_of(me * slim, slim)
    temporal = (hidden_ref[:, pl.ds(start, slim)].astype(jnp.float32) + summed).astype(bf)
    temporal_ref[...] = temporal
    rows[0] = temporal
    row_swap = to_partner(0, rows.at[0], rows.at[1])
    row_swap.start()

    part = din.shape[2] // n
    share = headw.shape[2] // n
    lanes = dqkv.shape[3]

    def at_code(c):
        return slice(c * s_local, (c + 1) * s_local)

    def features(j):
        return pl.ds(pl.multiple_of(j * part, part), part)

    turns = order + [0]

    class Reduction:
        def __init__(self, phase, a, block_of, buf):
            self.phase, self.a, self.block_of, self.buf = phase, a, block_of, buf
            self.firsts = {}

        def send(self, stage, i, h, at, peer):
            spot_of = (self.a, i, at)
            copy = to_peer(
                2 * self.phase + stage, self.a if stage else 4 * i + 2 * h + self.a,
                self.buf.at[(2 * stage, *spot_of)], self.buf.at[(2 * stage + 1, *spot_of)], peer,
            )
            copy.start()
            return copy

        def start_one(self, i):
            target = lax.rem(spot + turns[i], half_n)
            self.buf[0, self.a, i] = self.block_of(2 * target + 1 - pair).astype(bf)
            for h, at in halves(self.buf.shape[3]):
                self.firsts[i, h] = self.send(0, i, h, at, mate)

        def forward_one(self, i):
            target = lax.rem(spot + turns[i], half_n)
            block = self.block_of(2 * target + pair)
            added = []
            for h, at in halves(self.buf.shape[3]):
                self.firsts[i, h].wait_recv()
                added.append(block[at] + self.buf[1, self.a, i, at].astype(jnp.float32))
                if turns[i]:
                    self.buf[2, self.a, i, at] = added[-1].astype(bf)
                    self.send(1, i, h, at, 2 * target + pair)
            self.own = jnp.concatenate(added, axis=0)

        def start(self):
            for i in range(half_n):
                self.start_one(i)

        def forward(self):
            for i in range(half_n):
                self.forward_one(i)

        def result(self):
            block = self.own
            all_came(2 * self.phase + 1, self.a, self.buf.at[3, self.a, pl.ds(0, half_n - 1)])
            for i in range(half_n - 1):
                block = block + self.buf[3, self.a, i].astype(jnp.float32)
            return block

        def drain(self):
            all_sent(2 * self.phase, self.buf.at[0, self.a])
            all_sent(2 * self.phase + 1, self.buf.at[2, self.a, pl.ds(0, half_n - 1)])

    def entry_block(a):
        def block_of(j):
            terms = [product(rows[a], din[c, :, features(j)]) for c in range(codes)]
            return ent[a, :, features(j)] + jnp.concatenate(terms, axis=0)
        return block_of

    def row_squares(block):
        return lax.dot_general(
            jnp.ones((8, part), jnp.float32), block * block, (((1,), (1,)), ((), ())),
            preferred_element_type=jnp.float32, precision=lax.Precision.HIGHEST,
        )

    def squares_out(which, a, block):
        squares[which, a, me] = row_squares(block)
        for d in range(1, n):
            to_peer(
                8 + which + 4 * a, 0, squares.at[which, a, me], squares.at[which, a, me],
                lax.rem(me + d, n),
            ).start()

    def row_factor(which, a):
        all_came(8 + which + 4 * a, 0, squares.at[which, a, pl.ds(0, n - 1)])
        mean = jnp.sum(squares[which, a], axis=0) / (n * part)
        column = lax.dot_general(
            mean, jnp.full((8, 128), 0.125, jnp.float32), (((0,), (0,)), ((), ())),
            preferred_element_type=jnp.float32, precision=lax.Precision.HIGHEST,
        )
        return lax.rsqrt(column + EPSILON)

    class Gather:
        def __init__(self, a):
            self.a = a
            self.copies = []

        def send(self, phase, d, place, at, peer):
            there = nrm.at[place, self.a, at]
            copy = to_peer(phase, d, there, there, peer)
            copy.start()
            return copy

        def start(self, block):
            nrm[me, self.a] = (block * dgain_ref[:, features(me)]).astype(bf)
            for i, d in enumerate(order):
                peer = 2 * lax.rem(spot + d, half_n) + pair
                for h, at in halves(nrm.shape[2]):
                    self.copies.append(self.send(6, 4 * i + 2 * h + self.a, me, at, peer))
            self.send(7, self.a, me, slice(None), mate)

        def forward_one(self, i):
            came = 2 * lax.rem(spot - order[i] + half_n, half_n) + pair
            for h, at in halves(nrm.shape[2]):
                self.copies[2 * i + h].wait_recv()
                self.send(7, self.a, came, at, mate)

        def forward(self):
            for i in range(half_n - 1):
                self.forward_one(i)

    def projections(a, r):
        all_came(7, a, nrm.at[pl.ds(0, half_n), a])
        chunk = lax.rem(a + sec, 2)
        for c in range(codes):
            x = jnp.concatenate([nrm[j, a, at_code(c), :] for j in range(n)], axis=1)
            f = r[at_code(c)]
            qs[chunk, c] = (product(x, dqkv[c, 0]) * f).astype(bf)
            kvs[chunk, 0, c] = (product(x, dqkv[c, 1]) * f).astype(bf)
            kvs[chunk, 1, c] = (product(x, dqkv[c, 2]) * f).astype(bf)
        to_partner(1 + chunk, kvs.at[chunk], kvr.at[chunk]).start()

    row_head = lax.rem(lax.broadcasted_iota(jnp.int32, (2 * lanes, lanes), 0), lanes) // DEPTH_HDIM
    col_head = lax.broadcasted_iota(jnp.int32, (2 * lanes, lanes), 1) // DEPTH_HDIM
    ones = jnp.where(row_head == col_head, 1.0, 0.0).astype(bf)
    scale = 1.0 / math.sqrt(DEPTH_HDIM)

    def scores(queries, keys):
        both = jnp.concatenate(
            [query * key.astype(jnp.float32) for query, key in zip(queries, keys)], axis=0
        )
        high = both.astype(bf)
        low = (both - high.astype(jnp.float32)).astype(bf)
        out = product(jnp.concatenate([high, low], axis=1), ones) * scale
        return [out[i * s_local:(i + 1) * s_local] for i in range(len(queries))]

    partner_swaps = [row_swap]

    def attention(a):
        queries = [qs[a, c].astype(jnp.float32) for c in range(codes)]
        pairs = [(q, k) for q in range(codes) for k in range(q + 1)]
        local = scores([queries[q] for q, _ in pairs], [kvs[a, 0, k] for _, k in pairs])
        local = dict(zip(pairs, local))
        swap = to_partner(1 + a, kvs.at[a], kvr.at[a])
        swap.wait_recv()
        partner_swaps.append(swap)
        pairs = [(q, k) for q in range(codes) for k in range(codes)]
        prior = scores([queries[q] for q, _ in pairs], [kvr[a, 0, k] for _, k in pairs])
        prior = dict(zip(pairs, prior))
        for q in range(codes):
            every = [jnp.where(sec > 0, prior[q, k], -jnp.inf) for k in range(codes)]
            every += [local[q, k] for k in range(q + 1)]
            top = every[0]
            for item in every[1:]:
                top = jnp.maximum(top, item)
            expo = [jnp.exp(item - top) for item in every]
            sums = expo[0]
            for item in expo[1:]:
                sums = sums + item
            out = None
            for k, item in enumerate(expo):
                value = kvr[a, 1, k] if k < codes else kvs[a, 1, k - codes]
                term = (item / sums).astype(bf).astype(jnp.float32) * value.astype(jnp.float32)
                out = term if out is None else out + term
            mix[a, at_code(q), :] = out.astype(bf)

    def resid_block(a):
        def block_of(j):
            return jnp.concatenate(
                [product(mix[a, at_code(c), :], dout[c, :, features(j)]) for c in range(codes)],
                axis=0,
            )
        return block_of

    def vocab_block(hidden):
        def block_of(j):
            there = pl.ds(pl.multiple_of(j * share, share), share)
            return jnp.concatenate(
                [product(hidden[at_code(c), :], headw[c, :, there]) for c in range(codes)],
                axis=0,
            )
        return block_of

    entries = [Reduction(1, a, entry_block(a), ebuf) for a in range(2)]
    entries[0].start()
    row_swap.wait_recv()
    for i in range(half_n):
        entries[1].start_one(i)
        if i:
            entries[0].forward_one(i - 1)
    entries[0].forward_one(half_n - 1)
    entries[1].forward()
    gathers = [Gather(a) for a in range(2)]
    for a in range(2):
        block = entries[a].result()
        gathers[a].start(block)
        squares_out(0, a, block)
        entry[lax.rem(a + sec, 2)] = block
    gathers[0].forward()
    for i in range(half_n - 1):
        if i == half_n - 2:
            factor = row_factor(0, 0)
        gathers[1].forward_one(i)
    loads["dqkv"].wait()
    loads["dout"].wait()
    for a in range(2):
        if a:
            factor = row_factor(0, a)
        projections(a, factor)
    resids = [Reduction(2, a, resid_block(a), dbuf) for a in range(2)]
    for a in range(2):
        attention(a)
        resids[a].start()
    resids[0].forward()
    resids[1].forward()
    loads["headw"].wait()
    heads_of = []
    for a in range(2):
        resid = entry[a] + resids[a].result()
        if a:
            squares_out(1, a, resid)
        hidden = (resid * hgain_ref[:, features(me)]).astype(bf)
        heads_of.append(Reduction(5, a, vocab_block(hidden), lbuf))
        heads_of[a].start()
        if not a:
            squares_out(1, a, resid)
    heads_of[0].forward()
    heads_of[1].forward()
    factors = [row_factor(1, a) for a in range(2)]
    for a in range(2):
        out = heads_of[a].result() * factors[a][:, :1]
        logits_ref[:, a * s_local:(a + 1) * s_local, :] = out.reshape(codes, s_local, share)
    all_sent(0, tbuf.at[0])
    all_sent(1, tbuf.at[2, pl.ds(0, half_n - 1)])
    for item in entries + resids + heads_of:
        item.drain()
    all_sent(6, nrm.at[pl.ds(0, half_n - 1)])
    all_sent(7, nrm.at[pl.ds(0, half_n)])
    for which in range(2):
        for a in range(2):
            all_sent(8 + which + 4 * a, squares.at[which, a, pl.ds(0, n - 1)])
    for copy in partner_swaps:
        copy.wait_send()
    assert len(arrivals) <= recv_sem.shape[0]


def deliver_kernel(temporal_ref, logits_ref, temporal_hbm, logits_hbm, turned, sems):
    first = pltpu.make_async_copy(temporal_ref, temporal_hbm, sems.at[0])
    first.start()
    turned[...] = jnp.swapaxes(logits_ref[...], 0, 1)
    second = pltpu.make_async_copy(turned, logits_hbm, sems.at[1])
    second.start()
    first.wait()
    second.wait()


def fused(
    n, hidden_in, temporal_gain, temporal_qkv, temporal_out_weight, cache_keys, cache_values,
    lengths, depth_in, depth_embed, depth_gain, depth_qkv, depth_out_weight, head_gain,
    head_weight, tokens,
):
    s_local, width = hidden_in.shape
    codes, slim, deep = depth_in.shape
    streams = 2 * s_local
    total = codes * streams
    lanes = depth_qkv.shape[3]
    part = head_weight.shape[1]
    share = head_weight.shape[2] // n
    bf, f32 = jnp.bfloat16, jnp.float32
    pieces = 4
    big = [temporal_qkv, cache_keys, cache_values, temporal_out_weight, depth_in, depth_embed,
           depth_qkv, depth_out_weight, head_weight]
    small = [hidden_in, temporal_gain[None, :], lengths[None, :], tokens.T, depth_gain[None, :],
             head_gain[None, :]]
    vmem = pl.BlockSpec(memory_space=pltpu.VMEM)
    scratch = [pltpu.VMEM(a.shape, a.dtype) for a in small + big] + [
        pltpu.VMEM((4, n // 2, s_local, slim), bf),
        pltpu.VMEM((2, s_local, slim), bf),
        pltpu.VMEM((2, total // 2, deep), f32),
        pltpu.VMEM((4, 2, n // 2, total // 2, part), bf),
        pltpu.VMEM((n, 2, total // 2, part), bf),
        pltpu.VMEM((2, 2, codes, s_local, lanes), bf),
        pltpu.VMEM((2, 2, codes, s_local, lanes), bf),
        pltpu.VMEM((2, total // 2, lanes), bf),
        pltpu.VMEM((4, 2, n // 2, total // 2, part), bf),
        pltpu.VMEM((4, 2, n // 2, total // 2, share), bf),
        pltpu.VMEM((2, 2, n, 8, total // 2), f32),
        pltpu.VMEM((2, codes, s_local, lanes), bf),
        pltpu.VMEM((2, total // 2, part), f32),
        pltpu.SemaphoreType.DMA((3 * pieces + 13 + n,)),
        pltpu.SemaphoreType.DMA((14,)),
        pltpu.SemaphoreType.DMA((8 * n + 2,)),
        pltpu.SemaphoreType.DMA((3,)),
        pltpu.SemaphoreType.DMA((3,)),
    ]
    temporal, logits = pl.pallas_call(
        functools.partial(tick_kernel, n, pieces),
        out_shape=(
            pltpu.VMEM((s_local, slim), bf),
            pltpu.VMEM((codes, streams, share), f32),
        ),
        in_specs=[pl.BlockSpec(memory_space=pl.ANY)] * 15,
        out_specs=(vmem, vmem),
        scratch_shapes=scratch,
        compiler_params=pltpu.CompilerParams(
            collective_id=0, has_side_effects=True, vmem_limit_bytes=60 * 1024 * 1024
        ),
    )(
        *small, *big,
    )
    return pl.pallas_call(
        deliver_kernel,
        out_shape=(
            jax.ShapeDtypeStruct((s_local, slim), bf),
            jax.ShapeDtypeStruct((streams, codes, share), f32),
        ),
        in_specs=[vmem] * 2,
        out_specs=(pl.BlockSpec(memory_space=pl.ANY),) * 2,
        scratch_shapes=[
            pltpu.VMEM((streams, codes, share), f32),
            pltpu.SemaphoreType.DMA((2,)),
        ],
        compiler_params=pltpu.CompilerParams(vmem_limit_bytes=2 * 1024 * 1024),
    )(temporal, logits)


def fits(n, arrays):
    hidden_in, depth_in, depth_qkv = arrays[0], arrays[7], arrays[10]
    total = depth_in.shape[0] * 2 * hidden_in.shape[0]
    return (
        lax.axis_size("section") == 2
        and depth_qkv.shape[3] == 128
        and arrays[13].shape[1] % 128 == 0
        and arrays[13].shape[2] % (128 * n) == 0
        and n % 2 == 0
        and total % 256 == 0
        and hidden_in.shape[0] % 16 == 0
        and arrays[4].shape[1] <= HEAD_DIM
        and arrays[2].shape[2] <= 8 * HEAD_DIM
    )


def any_size(*arrays):
    n = lax.axis_size("tp")
    if fits(n, arrays):
        return fused(n, *arrays)
    return per_device(*arrays)


def solution(mesh):
    return jax.shard_map(
        any_size,
        mesh=mesh,
        in_specs=(
            P(("grp", "section"), None),
            P(),
            P(None, None, "tp"),
            P("tp", None),
            P(("grp", "section"), None, "tp"),
            P(("grp", "section"), None, "tp"),
            P(("grp", "section")),
            P("section", "tp", None),
            P("section", "tp", None),
            P(),
            P("section", None, None, "tp"),
            P("section", "tp", None),
            P(),
            P("section", "tp", None),
            P("grp", "section"),
        ),
        out_specs=(P(("grp", "section"), "tp"), P("grp", "section", "tp")),
        check_vma=False,
    )
```
